32 devices in a mesh: fsdp: 4 (over z), ctx: 2 (over core), tp: 4 (over y, x).
Axes of the slice: x: 2, y: 2, z: 4, core: 2. Of those that a mesh axis runs over, the one named last changes fastest.
Arguments:
- tokens: bfloat16 [16, 1024, 768], P('fsdp', 'ctx'), may hold values from -6 to 6
- lengths: int32 [16], P('fsdp'), may hold values from 256 to 1024, as said below
- qkv_weight: bfloat16 [3, 768, 768], P(None, 'fsdp', 'tp'), may hold values from -0.21875 to 0.21875
- qv_bias: float32 [2, 768], P(None, 'tp'), may hold values from -3 to 3
- out_weight: bfloat16 [768, 768], P('tp', 'fsdp'), may hold values from -1.75 to 1.75
- out_bias: float32 [768], replicated, may hold values from -3 to 3
- ffn_in: bfloat16 [768, 3072], P('fsdp', 'tp'), may hold values from -0.21875 to 0.21875
- ffn_in_bias: float32 [3072], P('tp'), may hold values from -3 to 3
- ffn_out: bfloat16 [3072, 768], P('tp', 'fsdp'), may hold values from -0.109375 to 0.109375
- ffn_out_bias: float32 [768], replicated, may hold values from -3 to 3
- norm_gains: float32 [2, 768], replicated, may hold values from 0.1 to 1.9
- norm_shifts: float32 [2, 768], replicated, may hold values from -3 to 3
- cotangent: bfloat16 [16, 1024, 768], P('fsdp', 'ctx'), may hold values from -6 to 6
Outputs:
- layer_output: bfloat16 [16, 1024, 768], P('fsdp', 'ctx')
- grad_tokens: float32 [16, 1024, 768], P('fsdp', 'ctx')
- grad_qkv_weight: float32 [3, 768, 768], P(None, 'fsdp', 'tp')
- grad_qv_bias: float32 [2, 768], P(None, 'tp')
- grad_out_weight: float32 [768, 768], P('tp', 'fsdp')
- grad_out_bias: float32 [768], replicated
- grad_ffn_in: float32 [768, 3072], P('fsdp', 'tp')
- grad_ffn_in_bias: float32 [3072], P('tp')
- grad_ffn_out: float32 [3072, 768], P('tp', 'fsdp')
- grad_ffn_out_bias: float32 [768], replicated
- grad_norm_gains: float32 [2, 768], replicated
- grad_norm_shifts: float32 [2, 768], replicated
The draws below stay inside these ranges and needn't reach their ends.
Inputs may be any that keep to these rules, and one draw needn't show every extreme that they name: `lengths`: positions at or past a sequence's length are padding. Some sequence has exactly 1024 valid tokens and another exactly 256.
All inputs are finite; a program needn't handle non-finite values.
Results may differ from the reference program's by a relative error of at most 0.02.
Values may be sent and summed in bfloat16 or wider, within the bound.
No kernel may reach another device: no remote copies, remote signals or barrier semaphores. Data moves between devices by JAX's collectives and lax.ppermute only.
A program may use at most 192 MiB of HBM per device.

```python
import jax
import jax.numpy as jnp
from jax import lax

D = 768
HEADS = 12
HD = 64
FF = 3072
LEN = 1024
SEQS = 16


def draw_lengths(key, part):
    first, second, third = jax.random.split(key, 3)
    lengths_base = jax.random.randint(first, (SEQS,), LEN // 4, LEN + 1)
    longest = jax.random.randint(second, (), 0, SEQS)
    offset = jax.random.randint(third, (), 1, SEQS)
    shortest = (longest + offset) % SEQS
    lengths_base = lengths_base.at[longest].set(LEN)
    lengths_base = lengths_base.at[shortest].set(LEN // 4)
    return lengths_base.astype(jnp.int32)


def raised(drawn, key, source, target, blocks, factor):
    owner, partner = [(jnp.arange(drawn.shape[dim]) // (drawn.shape[dim] // blocks)).reshape([-1 if axis == dim else 1 for axis in range(drawn.ndim)]) for dim in (source, target)]
    chosen = jax.random.permutation(key, blocks)[partner]
    strong = (owner == chosen) | (owner == (partner + blocks // 2) % blocks)
    return jnp.where(strong, factor * drawn, drawn)


def levels(own_key, dims, cuts, low, largest):
    gain = 1.0
    for axis_at, blocks in cuts:
        draws = jax.random.uniform(jax.random.fold_in(jax.random.fold_in(own_key, 6), axis_at), (blocks,), jnp.float32, low / len(cuts), largest / len(cuts))
        gain = gain * jnp.repeat(jnp.exp(draws), dims[axis_at] // blocks).reshape((-1,) + (1,) * (len(dims) - 1 - axis_at))
    return gain


def noise(rng, extent, scale, limit, shards=(), held_as=jnp.bfloat16):
    array = jax.random.normal(rng, extent, jnp.float32) * scale
    if len(shards) > 0:
        array = levels(rng, extent, shards, -0.22, 0.18) * array
    return jnp.clip(array, min=-limit, max=limit).astype(held_as)


def heavy_noise(stream_key, shape, scale, limit, cuts, heavy, kind=jnp.bfloat16):
    entries = scale * jax.random.normal(stream_key, shape, jnp.float32)
    if cuts:
        entries = entries * levels(stream_key, shape, cuts, -0.22, 0.18)
    return jnp.clip(raised(entries, jax.random.fold_in(stream_key, 3), *heavy), -limit, limit).astype(kind)


def setup_inputs(seed: int = 0) -> dict:
    key_list = jax.random.split(jax.random.key(seed), 14)
    return {
        "tokens": heavy_noise(key_list[0], (SEQS, LEN, D), 1.0, 6.0, ((0, 4), (1, 2)), (0, 2, 4, 2.0)),
        "lengths": draw_lengths(jax.random.fold_in(key_list[13], 71), 0),
        "qkv_weight": noise(key_list[2], (3, D, D), D ** -0.5, 0.21875, ((1, 4), (2, 4))),
        "qv_bias": noise(key_list[3], (2, D), 0.5, 3.0, ((1, 4),), jnp.float32),
        "out_weight": noise(key_list[4], (D, D), (D // 64) ** -0.5, 1.75, ((0, 4), (1, 4))),
        "out_bias": noise(key_list[5], (D,), 0.5, 3.0, (), jnp.float32),
        "ffn_in": noise(key_list[6], (D, FF), D ** -0.5, 0.21875, ((0, 4), (1, 4))),
        "ffn_in_bias": noise(key_list[7], (FF,), 0.5, 3.0, ((0, 4),), jnp.float32),
        "ffn_out": noise(key_list[8], (FF, D), FF ** -0.5, 0.109375, ((0, 4), (1, 4))),
        "ffn_out_bias": noise(key_list[9], (D,), 0.5, 3.0, (), jnp.float32),
        "norm_gains": jnp.clip(1.0 + 0.18 * jax.random.normal(key_list[10], (2, D), jnp.float32), 0.1, 1.9),
        "norm_shifts": noise(key_list[11], (2, D), 0.5, 3.0, (), jnp.float32),
        "cotangent": heavy_noise(key_list[12], (SEQS, LEN, D), 1.0, 6.0, ((0, 4), (1, 2)), (0, 2, 4, 2.0)),
    }


@jax.custom_vjp
def low(v):
    return lax.optimization_barrier(v.astype(jnp.bfloat16)).astype(jnp.float32)

@jax.custom_vjp
def low_back(v):
    return v

def low_keep(v):
    return (low(v), None)

def low_pass(kept, grad):
    return (grad,)

def back_keep(v):
    return (v, None)

def back_low(kept, grad):
    return (low(grad),)
low.defvjp(low_keep, low_pass)
low_back.defvjp(back_keep, back_low)

def matmul_hi(left, right):
    return jnp.dot(left, right, precision=lax.Precision.HIGHEST)

def layer_norm(residual, gain_row, shift_row):
    center = lax.optimization_barrier(jnp.mean(residual, axis=-1, keepdims=True))
    centred = residual - center
    spread = lax.optimization_barrier(jnp.mean(centred * centred, axis=-1, keepdims=True))
    return centred * lax.rsqrt(spread + 1e-05) * gain_row + shift_row

def one_sequence(inputs, length, params):
    qkv_weight, qv_bias, out_weight, out_bias, ffn_in, ffn_in_bias, ffn_out, ffn_out_bias, norm_gains, norm_shifts = params
    queries = low_back(low(matmul_hi(inputs, qkv_weight[0]) + qv_bias[0]))
    keys_all = low_back(low(matmul_hi(inputs, qkv_weight[1])))
    values_all = low_back(low(matmul_hi(inputs, qkv_weight[2]) + qv_bias[1]))
    query_heads = queries.reshape(LEN, HEADS, HD)
    key_heads = keys_all.reshape(LEN, HEADS, HD)
    value_heads = values_all.reshape(LEN, HEADS, HD)
    dot_scores = low_back(jnp.einsum('qhd,khd->hqk', query_heads, key_heads, precision=lax.Precision.HIGHEST))
    key_valid = jnp.arange(LEN, dtype=jnp.int32) < length
    scores = jnp.where(key_valid[None, None, :], dot_scores * 0.125, -1000000000.0)
    weights_soft = low(jax.nn.softmax(scores, axis=-1))
    context = jnp.einsum('hqk,khd->qhd', weights_soft, value_heads, precision=lax.Precision.HIGHEST)
    context = low_back(low(context.reshape(LEN, D)))
    attended = low_back(matmul_hi(context, out_weight) + out_bias)
    normed = layer_norm(inputs + attended, norm_gains[0], norm_shifts[0])
    hidden = low_back(matmul_hi(low(normed), ffn_in) + ffn_in_bias)
    activated = low(jax.nn.gelu(hidden, approximate=False))
    branch = low_back(matmul_hi(activated, ffn_out) + ffn_out_bias)
    return layer_norm(normed + branch, norm_gains[1], norm_shifts[1])

def reference(tokens, lengths, qkv_weight, qv_bias, out_weight, out_bias, ffn_in, ffn_in_bias, ffn_out, ffn_out_bias, norm_gains, norm_shifts, cotangent):
    params = tuple((element.astype(jnp.float32) for element in (qkv_weight, qv_bias, out_weight, out_bias, ffn_in, ffn_in_bias, ffn_out, ffn_out_bias, norm_gains, norm_shifts)))
    inputs = tokens.astype(jnp.float32)

    def forward(inputs_all, params_all):
        one_block = jax.checkpoint(one_sequence)

        def advance(carried, element):
            return (carried, one_block(element[0], element[1], params_all))
        _, result = lax.scan(advance, jnp.zeros((), jnp.float32), (inputs_all, lengths))
        return result
    output, pullback = jax.vjp(forward, inputs, params)
    valid_rows = (jnp.arange(LEN, dtype=jnp.int32)[None, :] < lengths[:, None]).astype(jnp.float32)
    grad_inputs, grads = pullback(cotangent.astype(jnp.float32) * valid_rows[:, :, None])
    return (output.astype(jnp.bfloat16), grad_inputs, grads[0], grads[1], grads[2], grads[3], grads[4], grads[5], grads[6], grads[7], grads[8], grads[9])
```

```python
import functools
import math

import jax
import jax.numpy as jnp
from jax import lax
from jax.experimental import pallas as pl
from jax.experimental.pallas import tpu as pltpu
from jax.sharding import PartitionSpec as P

HD = 64
EPS = 1e-05
MASKED = -1000000000.0
LOG2E = math.log2(math.e)
SCALE = 0.125
BF = jnp.bfloat16
F32 = jnp.float32
VMEM_LIMIT = 60 * 1024 * 1024

X_SWAP = [(0, 1), (1, 0), (2, 3), (3, 2)]
Y_SWAP = [(0, 2), (2, 0), (1, 3), (3, 1)]
C_SWAP = [(0, 1), (1, 0)]


def nn(a, b):
    return lax.dot_general(a, b, (((1,), (0,)), ((), ())), preferred_element_type=F32)


def nt(a, b):
    return lax.dot_general(a, b, (((1,), (1,)), ((), ())), preferred_element_type=F32)


def tn(a, b):
    return lax.dot_general(a, b, (((0,), (0,)), ((), ())), preferred_element_type=F32)


def params(n=1):
    return pltpu.CompilerParams(
        dimension_semantics=("arbitrary",) * n, vmem_limit_bytes=VMEM_LIMIT
    )


def cost(flops, moved, trans=0):
    return pl.CostEstimate(flops=int(flops), bytes_accessed=int(moved), transcendentals=int(trans))


def spec(shape, index):
    return pl.BlockSpec(shape, index)


def whole(shape):
    zeros = (0,) * len(shape)
    return pl.BlockSpec(shape, lambda i, info: zeros)


def qkv_kernel(info, x_ref, a_ref, qb_ref, kvb_ref, q_ref, kv_ref):
    c = info[0]
    x = x_ref[...]
    kv_ref[0] = (nn(x, a_ref[c, 0]) + kvb_ref[0]).astype(BF)
    q_ref[0] = (nn(x, a_ref[1 - c, 0, :, 0 : q_ref.shape[2]]) + qb_ref[0]).astype(BF)


def qkv_call(info, x, wa, qb, kvb):
    rows, width = x.shape
    slots, half = wa.shape[1], wa.shape[3]
    feat = half // 2
    return pl.pallas_call(
        qkv_kernel,
        grid_spec=pltpu.PrefetchScalarGridSpec(
            num_scalar_prefetch=1,
            grid=(slots,),
            in_specs=[
                whole((rows, width)),
                spec((2, 1, width, half), lambda i, info: (0, i, 0, 0)),
                spec((1, 1, feat), lambda i, info: (i, 0, 0)),
                spec((1, 1, half), lambda i, info: (i, 0, 0)),
            ],
            out_specs=[
                spec((1, rows, feat), lambda i, info: (i, 0, 0)),
                spec((1, rows, half), lambda i, info: (i, 0, 0)),
            ],
        ),
        out_shape=[
            jax.ShapeDtypeStruct((slots, rows, feat), BF),
            jax.ShapeDtypeStruct((slots, rows, half), BF),
        ],
        compiler_params=params(),
        cost_estimate=cost(2 * rows * width * slots * 3 * feat, 8e6),
        name="qkv",
    )(info, x, wa, qb, kvb)


CHUNK = 256


def key_bias(info, rows, mine):
    owner = info[0] if mine else 1 - info[0]
    position = owner * rows + lax.broadcasted_iota(jnp.int32, (1, rows), 1)
    return jnp.where(position < info[1], 0.0, MASKED)


def attn_kernel(info, q_ref, kv_ref, kvo_ref, ctx_ref, lse_ref):
    rows, feat = q_ref.shape[1], q_ref.shape[2]
    heads = feat // HD
    bias_m, bias_o = key_bias(info, rows, True), key_bias(info, rows, False)
    step_rows = min(CHUNK, rows)
    lane = lax.broadcasted_iota(jnp.int32, (1, 128), 1)

    def chunk(n, carry):
        at = pl.ds(pl.multiple_of(n * step_rows, step_rows), step_rows)
        lse_all = jnp.zeros((step_rows, 128), F32)
        for h in range(heads):
            cols = slice(h * HD, (h + 1) * HD)
            vcols = slice(feat + h * HD, feat + (h + 1) * HD)
            q = q_ref[0, at, cols]
            s_m = nt(q, kv_ref[0, :, cols]) * (SCALE * LOG2E) + bias_m
            s_o = nt(q, kvo_ref[0, :, cols]) * (SCALE * LOG2E) + bias_o
            top = jnp.maximum(
                jnp.max(s_m, axis=1, keepdims=True), jnp.max(s_o, axis=1, keepdims=True)
            )
            e_m = jnp.exp2(s_m - top)
            e_o = jnp.exp2(s_o - top)
            total = jnp.sum(e_m, axis=1, keepdims=True) + jnp.sum(e_o, axis=1, keepdims=True)
            inv = 1.0 / total
            out = nn((e_m * inv).astype(BF), kv_ref[0, :, vcols]) + nn(
                (e_o * inv).astype(BF), kvo_ref[0, :, vcols]
            )
            ctx_ref[0, at, cols] = out.astype(BF)
            lse_all = jnp.where(lane == h, top + jnp.log2(total), lse_all)
        lse_ref[0, at, :] = lse_all
        return carry

    lax.fori_loop(0, rows // step_rows, chunk, 0)


def attn_call(info, q, kv, kvo):
    slots, rows, feat = q.shape
    half = kv.shape[2]
    blk = lambda w: spec((1, rows, w), lambda i, info: (i, 0, 0))
    heads = slots * feat // HD
    return pl.pallas_call(
        attn_kernel,
        grid_spec=pltpu.PrefetchScalarGridSpec(
            num_scalar_prefetch=1,
            grid=(slots,),
            in_specs=[blk(feat), blk(half), blk(half)],
            out_specs=[blk(feat), blk(128)],
        ),
        out_shape=[
            jax.ShapeDtypeStruct((slots, rows, feat), BF),
            jax.ShapeDtypeStruct((slots, rows, 128), F32),
        ],
        compiler_params=params(),
        cost_estimate=cost(
            16 * rows * rows * 2 * HD * heads, 8e6, 2 * rows * rows * heads
        ),
        name="attn",
    )(info, q, kv, kvo)


def attn_back_kernel(info, q_ref, kv_ref, kvo_ref, lse_ref, g_ref, gq_ref, gkv_ref, gkvo_ref, acc_m, acc_o):
    rows, feat = q_ref.shape[1], q_ref.shape[2]
    heads = feat // HD
    bias_m, bias_o = key_bias(info, rows, True), key_bias(info, rows, False)
    step_rows = min(CHUNK, rows)
    lane = lax.broadcasted_iota(jnp.int32, (1, 128), 1)
    acc_m[...] = jnp.zeros_like(acc_m)
    acc_o[...] = jnp.zeros_like(acc_o)

    def chunk(n, carry):
        at = pl.ds(pl.multiple_of(n * step_rows, step_rows), step_rows)
        lse_all = lse_ref[0, at, :]
        for h in range(heads):
            cols = slice(h * HD, (h + 1) * HD)
            vcols = slice(feat + h * HD, feat + (h + 1) * HD)
            q = q_ref[0, at, cols]
            g = g_ref[0, at, cols]
            lse = jnp.sum(jnp.where(lane == h, lse_all, 0.0), axis=1, keepdims=True)
            k_m, k_o = kv_ref[0, :, cols], kvo_ref[0, :, cols]
            p_m = jnp.exp2(nt(q, k_m) * (SCALE * LOG2E) + bias_m - lse)
            p_o = jnp.exp2(nt(q, k_o) * (SCALE * LOG2E) + bias_o - lse)
            gp_m = nt(g, kv_ref[0, :, vcols])
            gp_o = nt(g, kvo_ref[0, :, vcols])
            inner = jnp.sum(p_m * gp_m, axis=1, keepdims=True) + jnp.sum(
                p_o * gp_o, axis=1, keepdims=True
            )
            acc_m[:, vcols] += tn(p_m.astype(BF), g)
            acc_o[:, vcols] += tn(p_o.astype(BF), g)
            gs_m = (p_m * (gp_m - inner) * SCALE).astype(BF)
            gs_o = (p_o * (gp_o - inner) * SCALE).astype(BF)
            gq_ref[0, at, cols] = (nn(gs_m, k_m) + nn(gs_o, k_o)).astype(BF)
            acc_m[:, cols] += tn(gs_m, q)
            acc_o[:, cols] += tn(gs_o, q)
        return carry

    lax.fori_loop(0, rows // step_rows, chunk, 0)
    gkv_ref[0] = acc_m[...]
    gkvo_ref[0] = acc_o[...].astype(BF)


def attn_back_call(info, q, kv, kvo, lse, g):
    slots, rows, feat = q.shape
    half = kv.shape[2]
    blk = lambda w: spec((1, rows, w), lambda i, info: (i, 0, 0))
    heads = slots * feat // HD
    return pl.pallas_call(
        attn_back_kernel,
        grid_spec=pltpu.PrefetchScalarGridSpec(
            num_scalar_prefetch=1,
            grid=(slots,),
            in_specs=[blk(feat), blk(half), blk(half), blk(128), blk(feat)],
            out_specs=[blk(feat), blk(half), blk(half)],
            scratch_shapes=[pltpu.VMEM((rows, half), F32), pltpu.VMEM((rows, half), F32)],
        ),
        out_shape=[
            jax.ShapeDtypeStruct((slots, rows, feat), BF),
            jax.ShapeDtypeStruct((slots, rows, half), F32),
            jax.ShapeDtypeStruct((slots, rows, half), BF),
        ],
        compiler_params=params(),
        cost_estimate=cost(
            40 * rows * rows * 2 * HD * heads, 12e6, 2 * rows * rows * heads
        ),
        name="attn_back",
    )(info, q, kv, kvo, lse, g)


ROWS = 128


def row_mask(info, rows, start, count):
    position = info[0] * rows + start + lax.broadcasted_iota(jnp.int32, (count, 1), 0)
    return (position < info[1]).astype(F32)


def ffn_kernel(
    info, ctx_ref, wo_ref, x_ref, cot_ref, vec_ref, bin_ref, wb_ref, wc_ref,
    act_ref, slope_ref, nlow_ref, hat_ref, rstd_ref, out_ref, gb_ref, gr_ref, sums_ref,
    normed_sc, branch_sc,
):
    k = pl.program_id(0)
    rows, width = x_ref.shape
    slots, feat = ctx_ref.shape[0], ctx_ref.shape[2]

    @pl.when(k == 0)
    def _():
        def chunk(n, carry):
            at = pl.ds(pl.multiple_of(n * ROWS, ROWS), ROWS)
            res = x_ref[at, :].astype(F32) + vec_ref[0:1, :]
            for s in range(slots):
                res += nt(ctx_ref[s, at, :], wo_ref[0, s, :, feat : 2 * feat])
            center = jnp.mean(res, axis=1, keepdims=True)
            res = res - center
            rstd = lax.rsqrt(jnp.mean(res * res, axis=1, keepdims=True) + EPS)
            hat = res * rstd
            normed = hat * vec_ref[2:3, :] + vec_ref[4:5, :]
            hat_ref[at, :] = hat
            rstd_ref[at, :] = jnp.broadcast_to(rstd, (ROWS, 128))
            normed_sc[at, :] = normed
            nlow_ref[at, :] = normed.astype(BF)
            return carry

        lax.fori_loop(0, rows // ROWS, chunk, 0)

    def chunk(n, carry):
        at = pl.ds(pl.multiple_of(n * ROWS, ROWS), ROWS)
        u = nn(nlow_ref[at, :], wb_ref[0]) + bin_ref[0]
        cdf = 0.5 + 0.5 * lax.erf(u * math.sqrt(0.5))
        act = (u * cdf).astype(BF)
        act_ref[0, at, :] = act
        slope_ref[0, at, :] = cdf + u * (jnp.exp(u * u * -0.5) * (1.0 / math.sqrt(2.0 * math.pi)))
        part = nt(act, wc_ref[0])

        @pl.when(k == 0)
        def _():
            branch_sc[at, :] = part

        @pl.when(k > 0)
        def _():
            branch_sc[at, :] += part

        return carry

    lax.fori_loop(0, rows // ROWS, chunk, 0)

    @pl.when(k == pl.num_programs(0) - 1)
    def _():
        def chunk(n, carry):
            s_gain, s_shift, s_bias = carry
            at = pl.ds(pl.multiple_of(n * ROWS, ROWS), ROWS)
            res = normed_sc[at, :] + branch_sc[at, :] + vec_ref[1:2, :]
            center = jnp.mean(res, axis=1, keepdims=True)
            res = res - center
            rstd = lax.rsqrt(jnp.mean(res * res, axis=1, keepdims=True) + EPS)
            hat = res * rstd
            out_ref[at, :] = (hat * vec_ref[3:4, :] + vec_ref[5:6, :]).astype(BF)
            g = cot_ref[at, :].astype(F32) * row_mask(info, rows, n * ROWS, ROWS)
            s_shift += jnp.sum(g, axis=0, keepdims=True)
            s_gain += jnp.sum(g * hat, axis=0, keepdims=True)
            gh = g * vec_ref[3:4, :]
            gr = rstd * (
                gh
                - jnp.mean(gh, axis=1, keepdims=True)
                - hat * jnp.mean(gh * hat, axis=1, keepdims=True)
            )
            gr_ref[at, :] = gr
            gb = gr.astype(BF)
            gb_ref[at, :] = gb
            s_bias += jnp.sum(gb.astype(F32), axis=0, keepdims=True)
            return s_gain, s_shift, s_bias

        zero = jnp.zeros((1, width), F32)
        s_gain, s_shift, s_bias = lax.fori_loop(0, rows // ROWS, chunk, (zero, zero, zero))
        sums_ref[0:1, :] = s_gain
        sums_ref[1:2, :] = s_shift
        sums_ref[2:3, :] = s_bias
        sums_ref[3:8, :] = jnp.zeros((5, width), F32)


def ffn_call(info, ctx, wa, x, cot, vec, b_in, wb, wc):
    slots, rows, feat = ctx.shape
    width = x.shape[1]
    blocks, _, half = wb.shape
    kblk = lambda r, w: spec((1, r, w), lambda i, info: (i, 0, 0))
    return pl.pallas_call(
        ffn_kernel,
        grid_spec=pltpu.PrefetchScalarGridSpec(
            num_scalar_prefetch=1,
            grid=(blocks,),
            in_specs=[
                whole((slots, rows, feat)),
                spec((1, slots, width, half), lambda i, info: (1 - info[0], 0, 0, 0)),
                whole((rows, width)),
                whole((rows, width)),
                whole((8, width)),
                kblk(1, half),
                kblk(width, half),
                kblk(width, half),
            ],
            out_specs=[
                kblk(rows, half),
                kblk(rows, half),
                whole((rows, width)),
                whole((rows, width)),
                whole((rows, 128)),
                whole((rows, width)),
                whole((rows, width)),
                whole((rows, width)),
                whole((8, width)),
            ],
            scratch_shapes=[pltpu.VMEM((rows, width), F32), pltpu.VMEM((rows, width), F32)],
        ),
        out_shape=[
            jax.ShapeDtypeStruct((blocks, rows, half), BF),
            jax.ShapeDtypeStruct((blocks, rows, half), F32),
            jax.ShapeDtypeStruct((rows, width), BF),
            jax.ShapeDtypeStruct((rows, width), F32),
            jax.ShapeDtypeStruct((rows, 128), F32),
            jax.ShapeDtypeStruct((rows, width), BF),
            jax.ShapeDtypeStruct((rows, width), BF),
            jax.ShapeDtypeStruct((rows, width), F32),
            jax.ShapeDtypeStruct((8, width), F32),
        ],
        compiler_params=params(),
        cost_estimate=cost(4 * rows * width * blocks * half * 3, 3e7, 2 * rows * blocks * half),
        name="ffn",
    )(info, ctx, wa, x, cot, vec, b_in, wb, wc)


def down_kernel(info, gb_ref, act_ref, dc_ref, gt_sc):
    @pl.when(pl.program_id(0) == 0)
    def _():
        gt_sc[...] = gb_ref[...].T

    dc_ref[0] = nn(gt_sc[...], act_ref[0]).astype(BF)


def down_call(info, gb, act):
    rows, width = gb.shape
    blocks, _, half = act.shape
    kblk = lambda r, w: spec((1, r, w), lambda i, info: (i, 0, 0))
    return pl.pallas_call(
        down_kernel,
        grid_spec=pltpu.PrefetchScalarGridSpec(
            num_scalar_prefetch=1,
            grid=(blocks,),
            in_specs=[whole((rows, width)), kblk(rows, half)],
            out_specs=kblk(width, half),
            scratch_shapes=[pltpu.VMEM((width, rows), BF)],
        ),
        out_shape=jax.ShapeDtypeStruct((blocks, width, half), BF),
        compiler_params=params(),
        cost_estimate=cost(2 * rows * width * blocks * half, 9e6),
        name="down_grad",
    )(info, gb, act)


def ffn_back_kernel(
    info, gb_ref, slope_ref, wc_ref, wb_ref, nlow_ref, gr_ref, hat_ref, rstd_ref, vec_ref, wo_ref, ctx_ref,
    db_ref, dbin_ref, g1_ref, gatt_ref, gctx_ref, dwo_ref, sums_ref,
    nt_sc, acc_sc, gh_sc,
):
    k = pl.program_id(0)
    rows, width = gb_ref.shape
    half = wb_ref.shape[2]
    slots, feat = ctx_ref.shape[0], ctx_ref.shape[2]

    @pl.when(k == 0)
    def _():
        nt_sc[...] = nlow_ref[...].T

    def chunk(n, total):
        at = pl.ds(pl.multiple_of(n * ROWS, ROWS), ROWS)
        gh = (slope_ref[0, at, :] * nn(gb_ref[at, :], wc_ref[0])).astype(BF)
        gh_sc[at, :] = gh
        part = nt(gh, wb_ref[0])

        @pl.when(k == 0)
        def _():
            acc_sc[at, :] = part

        @pl.when(k > 0)
        def _():
            acc_sc[at, :] += part

        return total + jnp.sum(gh.astype(F32), axis=0, keepdims=True)

    dbin_ref[0] = lax.fori_loop(0, rows // ROWS, chunk, jnp.zeros((1, half), F32))
    db_ref[0] = nn(nt_sc[...], gh_sc[...]).astype(BF)

    @pl.when(k == pl.num_programs(0) - 1)
    def _():
        def chunk(n, carry):
            s_gain, s_shift, s_bias = carry
            at = pl.ds(pl.multiple_of(n * ROWS, ROWS), ROWS)
            g = acc_sc[at, :] + gr_ref[at, :]
            hat = hat_ref[at, :]
            s_shift += jnp.sum(g, axis=0, keepdims=True)
            s_gain += jnp.sum(g * hat, axis=0, keepdims=True)
            gh = g * vec_ref[2:3, :]
            g1 = rstd_ref[at, 0:1] * (
                gh
                - jnp.mean(gh, axis=1, keepdims=True)
                - hat * jnp.mean(gh * hat, axis=1, keepdims=True)
            )
            g1_ref[at, :] = g1
            gatt = g1.astype(BF)
            gatt_ref[at, :] = gatt
            s_bias += jnp.sum(gatt.astype(F32), axis=0, keepdims=True)
            for s in range(slots):
                gctx_ref[s, at, :] = nn(gatt, wo_ref[0, s, :, feat : 2 * feat]).astype(BF)
            return s_gain, s_shift, s_bias

        zero = jnp.zeros((1, width), F32)
        s_gain, s_shift, s_bias = lax.fori_loop(0, rows // ROWS, chunk, (zero, zero, zero))
        sums_ref[0:1, :] = s_gain
        sums_ref[1:2, :] = s_shift
        sums_ref[2:3, :] = s_bias
        sums_ref[3:8, :] = jnp.zeros((5, width), F32)
        nt_sc[...] = gatt_ref[...].T
        for s in range(slots):
            dwo_ref[s] = nn(nt_sc[...], ctx_ref[s]).astype(BF)


def ffn_back_call(info, gb, slope, wc, wb, nlow, gr, hat, rstd, vec, wa, ctx):
    slots, rows, feat = ctx.shape
    width = gb.shape[1]
    blocks, _, half = wb.shape
    kblk = lambda r, w: spec((1, r, w), lambda i, info: (i, 0, 0))
    return pl.pallas_call(
        ffn_back_kernel,
        grid_spec=pltpu.PrefetchScalarGridSpec(
            num_scalar_prefetch=1,
            grid=(blocks,),
            in_specs=[
                whole((rows, width)),
                kblk(rows, half),
                kblk(width, half),
                kblk(width, half),
                whole((rows, width)),
                whole((rows, width)),
                whole((rows, width)),
                whole((rows, 128)),
                whole((8, width)),
                spec((1, slots, width, half), lambda i, info: (1 - info[0], 0, 0, 0)),
                whole((slots, rows, feat)),
            ],
            out_specs=[
                kblk(width, half),
                kblk(1, half),
                whole((rows, width)),
                whole((rows, width)),
                whole((slots, rows, feat)),
                whole((slots, width, feat)),
                whole((8, width)),
            ],
            scratch_shapes=[
                pltpu.VMEM((width, rows), BF),
                pltpu.VMEM((rows, width), F32),
                pltpu.VMEM((rows, half), BF),
            ],
        ),
        out_shape=[
            jax.ShapeDtypeStruct((blocks, width, half), BF),
            jax.ShapeDtypeStruct((blocks, 1, half), F32),
            jax.ShapeDtypeStruct((rows, width), F32),
            jax.ShapeDtypeStruct((rows, width), BF),
            jax.ShapeDtypeStruct((slots, rows, feat), BF),
            jax.ShapeDtypeStruct((slots, width, feat), BF),
            jax.ShapeDtypeStruct((8, width), F32),
        ],
        compiler_params=params(),
        cost_estimate=cost(6 * rows * width * blocks * half, 3e7),
        name="ffn_back",
    )(info, gb, slope, wc, wb, nlow, gr, hat, rstd, vec, wa, ctx)


def qkv_back_kernel(
    info, x_ref, gq_ref, gkv_ref, gkvo_ref, wa_ref, dwo_ref, g1_ref,
    da_ref, gx_ref, sq_ref, skv_ref, xt_sc, acc_sc,
):
    s = pl.program_id(0)
    c = info[0]
    feat = gq_ref.shape[2]

    @pl.when(s == 0)
    def _():
        xt_sc[...] = x_ref[...].T
        acc_sc[...] = g1_ref[...]

    gkv = (gkv_ref[0] + gkvo_ref[0].astype(F32)).astype(BF)
    gq = gq_ref[0]
    da_ref[c, 0] = nn(xt_sc[...], gkv).astype(BF)
    da_ref[1 - c, 0, :, 0:feat] = nn(xt_sc[...], gq).astype(BF)
    da_ref[1 - c, 0, :, feat : 2 * feat] = dwo_ref[0]
    sq_ref[0] = jnp.sum(gq.astype(F32), axis=0, keepdims=True)
    skv_ref[0] = jnp.sum(gkv.astype(F32), axis=0, keepdims=True)
    acc_sc[...] += nt(gkv, wa_ref[c, 0]) + nt(gq, wa_ref[1 - c, 0, :, 0:feat])

    @pl.when(s == pl.num_programs(0) - 1)
    def _():
        gx_ref[...] = acc_sc[...].astype(BF)


def qkv_back_call(info, x, gq, gkv, gkvo, wa, dwo, g1):
    rows, width = x.shape
    slots, _, feat = gq.shape
    half = gkv.shape[2]
    blk = lambda r, w: spec((1, r, w), lambda i, info: (i, 0, 0))
    return pl.pallas_call(
        qkv_back_kernel,
        grid_spec=pltpu.PrefetchScalarGridSpec(
            num_scalar_prefetch=1,
            grid=(slots,),
            in_specs=[
                whole((rows, width)),
                blk(rows, feat),
                blk(rows, half),
                blk(rows, half),
                spec((2, 1, width, half), lambda i, info: (0, i, 0, 0)),
                blk(width, feat),
                whole((rows, width)),
            ],
            out_specs=[
                spec((2, 1, width, half), lambda i, info: (0, i, 0, 0)),
                whole((rows, width)),
                blk(1, feat),
                blk(1, half),
            ],
            scratch_shapes=[pltpu.VMEM((width, rows), BF), pltpu.VMEM((rows, width), F32)],
        ),
        out_shape=[
            jax.ShapeDtypeStruct((2, slots, width, half), BF),
            jax.ShapeDtypeStruct((rows, width), BF),
            jax.ShapeDtypeStruct((slots, 1, feat), F32),
            jax.ShapeDtypeStruct((slots, 1, half), F32),
        ],
        compiler_params=params(),
        cost_estimate=cost(4 * rows * width * slots * 3 * feat, 2e7),
        name="qkv_back",
    )(info, x, gq, gkv, gkvo, wa, dwo, g1)


def ring(size, step):
    return [(i, (i + step) % size) for i in range(size)]


def column_gather(shard, rank, size):
    if size > 4:
        return lax.all_gather(shard, "fsdp", axis=0, tiled=True)
    rows = shard.shape[0]
    full = jnp.zeros((size * rows,) + shard.shape[1:], shard.dtype)
    full = lax.dynamic_update_slice_in_dim(full, shard, rank * rows, 0)
    for step in range(1, size):
        got = lax.ppermute(shard, "fsdp", ring(size, step))
        full = lax.dynamic_update_slice_in_dim(full, got, ((rank - step) % size) * rows, 0)
    return full


def column_scatter(full, rank, size):
    rows = full.shape[0] // size
    if size > 4:
        return lax.psum_scatter(full, "fsdp", scatter_dimension=0, tiled=True).astype(F32)
    total = lax.dynamic_slice_in_dim(full, rank * rows, rows, 0).astype(F32)
    for step in range(1, size):
        piece = lax.dynamic_slice_in_dim(full, ((rank + step) % size) * rows, rows, 0)
        total = total + lax.ppermute(piece, "fsdp", ring(size, step)).astype(F32)
    return total


def plane_gather(mine):
    cut = mine.shape[0] // 2
    from_x = lax.ppermute(mine, "tp", X_SWAP)
    from_y = lax.ppermute(mine, "tp", Y_SWAP)
    upper = lax.ppermute(from_y[:cut], "tp", X_SWAP)
    lower = lax.ppermute(from_x[cut:], "tp", Y_SWAP)
    return mine, from_x, from_y, jnp.concatenate((upper, lower), axis=0)


def add(a, b):
    return (a.astype(F32) + b.astype(F32)).astype(BF)


def plane_scatter(blocks):
    cut = blocks.shape[1] // 2
    up, down = blocks[:, :cut], blocks[:, cut:]
    got = lax.ppermute(jnp.stack((up[1], up[3])), "tp", X_SWAP)
    mid_up = add(up[0], got[0])
    pass_up = add(up[2], got[1])
    got = lax.ppermute(jnp.stack((down[2], down[3])), "tp", Y_SWAP)
    mid_down = add(down[0], got[0])
    pass_down = add(down[1], got[1])
    upper = add(mid_up, lax.ppermute(pass_up, "tp", Y_SWAP))
    lower = add(mid_down, lax.ppermute(pass_down, "tp", X_SWAP))
    return jnp.concatenate((upper, lower), axis=0)


def weight_gather(shard, rank, size):
    column = column_gather(shard, rank, size)
    mine = jnp.stack(plane_gather(column))
    return jnp.stack((mine, lax.ppermute(mine, "ctx", C_SWAP)))


def weight_scatter(mine, other, rank, size):
    blocks = add(mine, lax.ppermute(other, "ctx", C_SWAP))
    return column_scatter(plane_scatter(blocks), rank, size).astype(BF)


def by_index(slots, index):
    swapped = jnp.where(index % 2 == 1, slots[jnp.array([1, 0, 3, 2])], slots)
    return jnp.where(index // 2 == 1, swapped[jnp.array([2, 3, 0, 1])], swapped)


def sum_everywhere(value, size):
    value = value + lax.ppermute(value, "ctx", C_SWAP)
    value = value + lax.ppermute(value, "tp", X_SWAP)
    value = value + lax.ppermute(value, "tp", Y_SWAP)
    step = 1
    while step < size:
        value = value + lax.ppermute(value, "fsdp", [(i, i ^ step) for i in range(size)])
        step *= 2
    return value


def place_sequences(slots, index, dtype):
    out = jnp.zeros((len(slots),) + slots[0].shape, dtype)
    for distance, block in enumerate(slots):
        out = lax.dynamic_update_slice(out, block.astype(dtype)[None], (index ^ distance, 0, 0))
    return out


def per_device(
    tokens, lengths, qkv_weight, qv_bias, out_weight, out_bias, ffn_in, ffn_in_bias,
    ffn_out, ffn_out_bias, norm_gains, norm_shifts, cotangent,
):
    size = lax.axis_size("fsdp")
    rank = lax.axis_index("fsdp")
    c = lax.axis_index("ctx")
    t = lax.axis_index("tp")
    seqs, rows, width = tokens.shape
    assert lax.axis_size("tp") == 4 and lax.axis_size("ctx") == 2 and seqs == 4
    feat = qkv_weight.shape[2]
    units = ffn_in.shape[1]
    half = units // 2
    assert half == 2 * feat
    x = lax.dynamic_index_in_dim(tokens, t, 0, keepdims=False)
    cot = lax.dynamic_index_in_dim(cotangent, t, 0, keepdims=False)
    length = lax.dynamic_index_in_dim(lengths, t, 0, keepdims=False)
    info = jnp.stack((c.astype(jnp.int32), length))

    shard_a = jnp.where(
        c == 0,
        jnp.concatenate((qkv_weight[1], qkv_weight[2]), axis=1),
        jnp.concatenate((qkv_weight[0], out_weight.T), axis=1),
    )
    shard_b = lax.dynamic_slice_in_dim(ffn_in, c * half, half, 1)
    shard_c = lax.dynamic_slice_in_dim(ffn_out, c * half, half, 0).T

    bias_own = jnp.concatenate((qv_bias.reshape(-1), ffn_in_bias)).reshape(1, -1)
    bias_x = lax.ppermute(bias_own, "tp", X_SWAP)
    bias_y = lax.ppermute(bias_own, "tp", Y_SWAP)
    bias_d = lax.ppermute(bias_x, "tp", Y_SWAP)
    bias = jnp.stack((bias_own, bias_x, bias_y, bias_d))
    q_bias = bias[:, :, :feat]
    kv_bias = jnp.concatenate((jnp.zeros_like(q_bias), bias[:, :, feat : 2 * feat]), axis=2)
    in_bias = bias[:, 0, 2 * feat :].reshape(4, 2, half).transpose(1, 0, 2)
    in_bias = jnp.where(c == 0, in_bias, in_bias[::-1]).reshape(8, 1, half)

    wa = weight_gather(shard_a, rank, size)
    wb = weight_gather(shard_b, rank, size).reshape(8, width, half)
    wc = weight_gather(shard_c, rank, size).reshape(8, width, half)
    zero_row = jnp.zeros_like(out_bias)
    vec = jnp.stack((out_bias, ffn_out_bias, norm_gains[0], norm_gains[1], norm_shifts[0], norm_shifts[1], zero_row, zero_row))

    q, kv = qkv_call(info, x, wa, q_bias, kv_bias)
    kv_other = lax.ppermute(kv, "ctx", C_SWAP)
    context, lse = attn_call(info, q, kv, kv_other)
    act, slope, nlow, hat, rstd, out, g_branch, g_r2, sums_two = ffn_call(
        info, context, wa, x, cot, vec, in_bias, wb, wc
    )
    layer_output = place_sequences(plane_gather(out), t, BF)
    dc = down_call(info, g_branch, act)
    own_c = weight_scatter(dc[:4], dc[4:], rank, size)
    db, d_in_bias, g_r1, g_att, g_context, dwo, sums_one = ffn_back_call(
        info, g_branch, slope, wc, wb, nlow, g_r2, hat, rstd, vec, wa, context
    )
    own_b = weight_scatter(db[:4], db[4:], rank, size)
    gq, gkv, gkv_send = attn_back_call(info, q, kv, kv_other, lse, g_context)
    gkv_got = lax.ppermute(gkv_send, "ctx", C_SWAP)
    da, g_tokens, sum_q, sum_kv = qkv_back_call(info, x, gq, gkv, gkv_got, wa, dwo, g_r1)
    own_a = weight_scatter(da[0], da[1], rank, size)
    grad_tokens = place_sequences(plane_gather(g_tokens), t, F32)

    own = jnp.stack((own_a, own_b, own_c))
    other = lax.ppermute(own, "ctx", C_SWAP)
    first = jnp.where(c == 0, own, other).astype(F32)
    second = jnp.where(c == 0, other, own).astype(F32)
    grad_qkv = jnp.stack((second[0][:, :feat], first[0][:, :feat], first[0][:, feat:]))
    grad_out = second[0][:, feat:].T
    grad_in = jnp.concatenate((first[1], second[1]), axis=1)
    grad_down = jnp.concatenate((first[2].T, second[2].T), axis=0)

    d_in = d_in_bias.reshape(2, 4, half)
    d_in = jnp.where(c == 0, d_in, d_in[::-1]).transpose(1, 0, 2).reshape(4, units)
    small = jnp.concatenate(
        (
            by_index(sum_q[:, 0], t).reshape(-1),
            by_index(sum_kv[:, 0, feat:], t).reshape(-1),
            by_index(d_in, t).reshape(-1),
            sums_one[:3].reshape(-1),
            sums_two[:3].reshape(-1),
        )
    ).reshape(-1, width)
    small = sum_everywhere(small, size)
    q_rows = 4 * feat // width
    at = 2 * q_rows
    d_q = lax.dynamic_slice_in_dim(small[:q_rows].reshape(-1), t * feat, feat, 0)
    d_v = lax.dynamic_slice_in_dim(small[q_rows:at].reshape(-1), t * feat, feat, 0)
    in_rows = 4 * units // width
    d_in_mine = lax.dynamic_slice_in_dim(small[at : at + in_rows].reshape(-1), t * units, units, 0)
    at += in_rows
    return (
        layer_output,
        grad_tokens,
        grad_qkv,
        jnp.stack((d_q, d_v)),
        grad_out,
        small[at + 2],
        grad_in,
        d_in_mine,
        grad_down,
        small[at + 5],
        jnp.stack((small[at], small[at + 3])),
        jnp.stack((small[at + 1], small[at + 4])),
    )


def solution(mesh):
    placed = (
        P("fsdp", "ctx", None),
        P("fsdp"),
        P(None, "fsdp", "tp"),
        P(None, "tp"),
        P("tp", "fsdp"),
        P(),
        P("fsdp", "tp"),
        P("tp"),
        P("tp", "fsdp"),
        P(),
        P(),
        P(),
        P("fsdp", "ctx", None),
    )
    return jax.shard_map(
        per_device,
        mesh=mesh,
        in_specs=placed,
        out_specs=(
            P("fsdp", "ctx", None),
            P("fsdp", "ctx", None),
            P(None, "fsdp", "tp"),
            P(None, "tp"),
            P("tp", "fsdp"),
            P(),
            P("fsdp", "tp"),
            P("tp"),
            P("tp", "fsdp"),
            P(),
            P(),
            P(),
        ),
        check_vma=False,
    )
```

```python
import functools
import math

import jax
import jax.numpy as jnp
from jax import lax
from jax.experimental import pallas as pl
from jax.experimental.pallas import tpu as pltpu
from jax.sharding import PartitionSpec as P

HD = 64
EPS = 1e-05
MASKED = -1000000000.0
LOG2E = math.log2(math.e)
SCALE = 0.125
BF = jnp.bfloat16
F32 = jnp.float32
MIB = 1024 * 1024

X_SWAP = [(0, 1), (1, 0), (2, 3), (3, 2)]
Y_SWAP = [(0, 2), (2, 0), (1, 3), (3, 1)]
C_SWAP = [(0, 1), (1, 0)]


def nn(a, b):
    return lax.dot_general(a, b, (((1,), (0,)), ((), ())), preferred_element_type=F32)


def nt(a, b):
    return lax.dot_general(a, b, (((1,), (1,)), ((), ())), preferred_element_type=F32)


def tn(a, b):
    return lax.dot_general(a, b, (((0,), (0,)), ((), ())), preferred_element_type=F32)


def params(mib):
    return pltpu.CompilerParams(
        dimension_semantics=("arbitrary",), vmem_limit_bytes=mib * MIB
    )


def cost(flops, moved, trans=0):
    return pl.CostEstimate(flops=int(flops), bytes_accessed=int(moved), transcendentals=int(trans))


def spec(shape, index):
    return pl.BlockSpec(shape, index)


def sequence(rows, width):
    return pl.BlockSpec((1, rows, width), lambda i, info: (info[2], 0, 0))


def whole(shape):
    zeros = (0,) * len(shape)
    return pl.BlockSpec(shape, lambda i, info: zeros)


def qkv_kernel(info, x_ref, a_ref, qb_ref, kvb_ref, q_ref, kv_ref):
    c = info[0]
    x = x_ref[0]
    kv_ref[0] = (nn(x, a_ref[c, 0]) + kvb_ref[0]).astype(BF)
    q_ref[0] = (nn(x, a_ref[1 - c, 0, :, 0 : q_ref.shape[2]]) + qb_ref[0]).astype(BF)


def qkv_call(info, x, wa, qb, kvb):
    _, rows, width = x.shape
    slots, half = wa.shape[1], wa.shape[3]
    feat = half // 2
    return pl.pallas_call(
        qkv_kernel,
        grid_spec=pltpu.PrefetchScalarGridSpec(
            num_scalar_prefetch=1,
            grid=(slots,),
            in_specs=[
                sequence(rows, width),
                spec((2, 1, width, half), lambda i, info: (0, i, 0, 0)),
                spec((1, 1, feat), lambda i, info: (i, 0, 0)),
                spec((1, 1, half), lambda i, info: (i, 0, 0)),
            ],
            out_specs=[
                spec((1, rows, feat), lambda i, info: (i, 0, 0)),
                spec((1, rows, half), lambda i, info: (i, 0, 0)),
            ],
        ),
        out_shape=[
            jax.ShapeDtypeStruct((slots, rows, feat), BF),
            jax.ShapeDtypeStruct((slots, rows, half), BF),
        ],
        compiler_params=params(12),
        cost_estimate=cost(2 * rows * width * slots * 3 * feat, 8e6),
        name="qkv",
    )(info, x, wa, qb, kvb)


def key_bias(info, rows, mine):
    owner = info[0] if mine else 1 - info[0]
    position = owner * rows + lax.broadcasted_iota(jnp.int32, (1, rows), 1)
    return jnp.where(position < info[1], 0.0, MASKED)


def attn_kernel(info, q_ref, kv_ref, kvo_ref, ctx_ref, lse_ref):
    rows, feat = q_ref.shape[1], q_ref.shape[2]
    bias_m, bias_o = key_bias(info, rows, True), key_bias(info, rows, False)
    lane = lax.broadcasted_iota(jnp.int32, (1, 128), 1)
    lse_all = jnp.zeros((rows, 128), F32)
    for h in range(feat // HD):
        cols = slice(h * HD, (h + 1) * HD)
        vcols = slice(feat + h * HD, feat + (h + 1) * HD)
        q = q_ref[0, :, cols]
        s_m = nt(q, kv_ref[0, :, cols]) * (SCALE * LOG2E) + bias_m
        s_o = nt(q, kvo_ref[0, :, cols]) * (SCALE * LOG2E) + bias_o
        top = jnp.maximum(
            jnp.max(s_m, axis=1, keepdims=True), jnp.max(s_o, axis=1, keepdims=True)
        )
        e_m = jnp.exp2(s_m - top)
        e_o = jnp.exp2(s_o - top)
        total = jnp.sum(e_m, axis=1, keepdims=True) + jnp.sum(e_o, axis=1, keepdims=True)
        out = nn(e_m.astype(BF), kv_ref[0, :, vcols]) + nn(e_o.astype(BF), kvo_ref[0, :, vcols])
        ctx_ref[0, :, cols] = (out * (1.0 / total)).astype(BF)
        lse_all = jnp.where(lane == h, top + jnp.log2(total), lse_all)
    lse_ref[0] = lse_all


def attn_call(info, q, kv, kvo):
    slots, rows, feat = q.shape
    half = kv.shape[2]
    blk = lambda w: spec((1, rows, w), lambda i, info: (i, 0, 0))
    heads = slots * feat // HD
    return pl.pallas_call(
        attn_kernel,
        grid_spec=pltpu.PrefetchScalarGridSpec(
            num_scalar_prefetch=1,
            grid=(slots,),
            in_specs=[blk(feat), blk(half), blk(half)],
            out_specs=[blk(feat), blk(128)],
        ),
        out_shape=[
            jax.ShapeDtypeStruct((slots, rows, feat), BF),
            jax.ShapeDtypeStruct((slots, rows, 128), F32),
        ],
        compiler_params=params(24),
        cost_estimate=cost(16 * rows * rows * 2 * HD * heads, 8e6, 2 * rows * rows * heads),
        name="attn",
    )(info, q, kv, kvo)


def attn_back_kernel(
    info, q_ref, kv_ref, kvo_ref, lse_ref, ctx_ref, g_ref, gq_ref, gkv_ref, gkvo_ref
):
    rows, feat = q_ref.shape[1], q_ref.shape[2]
    bias_m, bias_o = key_bias(info, rows, True), key_bias(info, rows, False)
    lane = lax.broadcasted_iota(jnp.int32, (1, 128), 1)
    lse_all = lse_ref[0]
    for h in range(feat // HD):
        cols = slice(h * HD, (h + 1) * HD)
        vcols = slice(feat + h * HD, feat + (h + 1) * HD)
        q, g = q_ref[0, :, cols], g_ref[0, :, cols]
        k_m, k_o = kv_ref[0, :, cols], kvo_ref[0, :, cols]
        lse = jnp.sum(jnp.where(lane == h, lse_all, 0.0), axis=1, keepdims=True)
        inner = jnp.sum(g.astype(F32) * ctx_ref[0, :, cols].astype(F32), axis=1, keepdims=True)
        p_m = jnp.exp2(nt(q, k_m) * (SCALE * LOG2E) + bias_m - lse)
        p_o = jnp.exp2(nt(q, k_o) * (SCALE * LOG2E) + bias_o - lse)
        gs_m = (p_m * (nt(g, kv_ref[0, :, vcols]) - inner)).astype(BF)
        gs_o = (p_o * (nt(g, kvo_ref[0, :, vcols]) - inner)).astype(BF)
        g_t, q_t = g.T, q.T
        gkv_ref[0, :, vcols] = nn(g_t, p_m.astype(BF)).T
        gkvo_ref[0, :, vcols] = nn(g_t, p_o.astype(BF)).T.astype(BF)
        gkv_ref[0, :, cols] = nn(q_t, gs_m).T * SCALE
        gkvo_ref[0, :, cols] = (nn(q_t, gs_o).T * SCALE).astype(BF)
        gq_ref[0, :, cols] = ((nn(gs_m, k_m) + nn(gs_o, k_o)) * SCALE).astype(BF)


def attn_back_call(info, q, kv, kvo, lse, ctx, g, first, slots):
    _, rows, feat = q.shape
    half = kv.shape[2]
    src = lambda w: spec((1, rows, w), lambda i, info: (i + first, 0, 0))
    blk = lambda w: spec((1, rows, w), lambda i, info: (i, 0, 0))
    heads = slots * feat // HD
    return pl.pallas_call(
        attn_back_kernel,
        grid_spec=pltpu.PrefetchScalarGridSpec(
            num_scalar_prefetch=1,
            grid=(slots,),
            in_specs=[src(feat), src(half), src(half), src(128), src(feat), src(feat)],
            out_specs=[blk(feat), blk(half), blk(half)],
        ),
        out_shape=[
            jax.ShapeDtypeStruct((slots, rows, feat), BF),
            jax.ShapeDtypeStruct((slots, rows, half), F32),
            jax.ShapeDtypeStruct((slots, rows, half), BF),
        ],
        compiler_params=params(24),
        cost_estimate=cost(40 * rows * rows * 2 * HD * heads, 12e6, 2 * rows * rows * heads),
        name="attn_back",
    )(info, q, kv, kvo, lse, ctx, g)


ROWS = 256


def wide(ref):
    return jnp.concatenate((ref[0, 0], ref[1, 0]), axis=1)


def row_mask(info, rows, start, count):
    position = info[0] * rows + start + lax.broadcasted_iota(jnp.int32, (count, 1), 0)
    return (position < info[1]).astype(F32)


def ffn_kernel(
    info, ctx_ref, wo_ref, x_ref, cot_ref, vec_ref, bin_ref, wb_ref, wc_ref,
    act_ref, slope_ref, nlow_ref, hat_ref, rstd_ref, out_ref, gb_ref, gr_ref, sums_ref,
    normed_sc, branch_sc,
):
    k = pl.program_id(0)
    _, rows, width = x_ref.shape
    slots, feat = ctx_ref.shape[0], ctx_ref.shape[2]

    @pl.when(k == 0)
    def _():
        def chunk(n, carry):
            at = pl.ds(pl.multiple_of(n * ROWS, ROWS), ROWS)
            res = x_ref[0, at, :].astype(F32) + vec_ref[0:1, :]
            for s in range(slots):
                res += nt(ctx_ref[s, at, :], wo_ref[0, s, :, feat : 2 * feat])
            center = jnp.mean(res, axis=1, keepdims=True)
            res = res - center
            rstd = lax.rsqrt(jnp.mean(res * res, axis=1, keepdims=True) + EPS)
            hat = res * rstd
            normed = hat * vec_ref[2:3, :] + vec_ref[4:5, :]
            hat_ref[at, :] = hat
            rstd_ref[at, :] = jnp.broadcast_to(rstd, (ROWS, 128))
            normed_sc[at, :] = normed
            nlow_ref[at, :] = normed.astype(BF)
            return carry

        lax.fori_loop(0, rows // ROWS, chunk, 0)

    u = nn(nlow_ref[...], wide(wb_ref)) + bin_ref[0]
    cdf = 0.5 + 0.5 * lax.erf(u * math.sqrt(0.5))
    act = (u * cdf).astype(BF)
    act_ref[0] = act
    slope_ref[0] = cdf + u * (jnp.exp(u * u * -0.5) * (1.0 / math.sqrt(2.0 * math.pi)))
    part = nt(act, wide(wc_ref))

    @pl.when(k == 0)
    def _():
        branch_sc[...] = part

    @pl.when(k > 0)
    def _():
        branch_sc[...] += part

    @pl.when(k == pl.num_programs(0) - 1)
    def _():
        def chunk(n, carry):
            s_gain, s_shift, s_bias = carry
            at = pl.ds(pl.multiple_of(n * ROWS, ROWS), ROWS)
            res = normed_sc[at, :] + branch_sc[at, :] + vec_ref[1:2, :]
            center = jnp.mean(res, axis=1, keepdims=True)
            res = res - center
            rstd = lax.rsqrt(jnp.mean(res * res, axis=1, keepdims=True) + EPS)
            hat = res * rstd
            out_ref[at, :] = (hat * vec_ref[3:4, :] + vec_ref[5:6, :]).astype(BF)
            g = cot_ref[0, at, :].astype(F32) * row_mask(info, rows, n * ROWS, ROWS)
            s_shift += jnp.sum(g, axis=0, keepdims=True)
            s_gain += jnp.sum(g * hat, axis=0, keepdims=True)
            gh = g * vec_ref[3:4, :]
            gr = rstd * (
                gh
                - jnp.mean(gh, axis=1, keepdims=True)
                - hat * jnp.mean(gh * hat, axis=1, keepdims=True)
            )
            gr_ref[at, :] = gr
            gb = gr.astype(BF)
            gb_ref[at, :] = gb
            s_bias += jnp.sum(gb.astype(F32), axis=0, keepdims=True)
            return s_gain, s_shift, s_bias

        zero = jnp.zeros((1, width), F32)
        s_gain, s_shift, s_bias = lax.fori_loop(0, rows // ROWS, chunk, (zero, zero, zero))
        sums_ref[0:1, :] = s_gain
        sums_ref[1:2, :] = s_shift
        sums_ref[2:3, :] = s_bias
        sums_ref[3:8, :] = jnp.zeros((5, width), F32)


def ffn_call(info, ctx, wa, x, cot, vec, b_in, wb, wc):
    slots, rows, feat = ctx.shape
    width = x.shape[2]
    blocks, half = wb.shape[1], wb.shape[3]
    units = 2 * half
    kblk = lambda r, w: spec((1, r, w), lambda i, info: (i, 0, 0))
    wblk = spec((2, 1, width, half), lambda i, info: (0, i, 0, 0))
    return pl.pallas_call(
        ffn_kernel,
        grid_spec=pltpu.PrefetchScalarGridSpec(
            num_scalar_prefetch=1,
            grid=(blocks,),
            in_specs=[
                whole((slots, rows, feat)),
                spec((1, slots, width, half), lambda i, info: (1 - info[0], 0, 0, 0)),
                sequence(rows, width),
                sequence(rows, width),
                whole((8, width)),
                kblk(1, units),
                wblk,
                wblk,
            ],
            out_specs=[
                kblk(rows, units),
                kblk(rows, units),
                whole((rows, width)),
                whole((rows, width)),
                whole((rows, 128)),
                whole((rows, width)),
                whole((rows, width)),
                whole((rows, width)),
                whole((8, width)),
            ],
            scratch_shapes=[pltpu.VMEM((rows, width), F32), pltpu.VMEM((rows, width), F32)],
        ),
        out_shape=[
            jax.ShapeDtypeStruct((blocks, rows, units), BF),
            jax.ShapeDtypeStruct((blocks, rows, units), F32),
            jax.ShapeDtypeStruct((rows, width), BF),
            jax.ShapeDtypeStruct((rows, width), F32),
            jax.ShapeDtypeStruct((rows, 128), F32),
            jax.ShapeDtypeStruct((rows, width), BF),
            jax.ShapeDtypeStruct((rows, width), BF),
            jax.ShapeDtypeStruct((rows, width), F32),
            jax.ShapeDtypeStruct((8, width), F32),
        ],
        compiler_params=params(28),
        cost_estimate=cost(12 * rows * width * blocks * units, 3e7, 2 * rows * blocks * units),
        name="ffn",
    )(info, ctx, wa, x, cot, vec, b_in, wb, wc)


def down_kernel(info, gb_ref, act_ref, dc_ref, gt_sc):
    @pl.when(pl.program_id(0) == 0)
    def _():
        gt_sc[...] = gb_ref[...].T

    grad = nn(gt_sc[...], act_ref[0]).astype(BF)
    half = dc_ref.shape[3]
    dc_ref[0, 0] = grad[:, :half]
    dc_ref[1, 0] = grad[:, half:]


def down_call(info, gb, act):
    rows, width = gb.shape
    blocks, _, units = act.shape
    half = units // 2
    return pl.pallas_call(
        down_kernel,
        grid_spec=pltpu.PrefetchScalarGridSpec(
            num_scalar_prefetch=1,
            grid=(blocks,),
            in_specs=[whole((rows, width)), spec((1, rows, units), lambda i, info: (i, 0, 0))],
            out_specs=spec((2, 1, width, half), lambda i, info: (0, i, 0, 0)),
            scratch_shapes=[pltpu.VMEM((width, rows), BF)],
        ),
        out_shape=jax.ShapeDtypeStruct((2, blocks, width, half), BF),
        compiler_params=params(16),
        cost_estimate=cost(2 * rows * width * blocks * units, 9e6),
        name="down_grad",
    )(info, gb, act)


def ffn_back_kernel(
    info, gb_ref, slope_ref, wc_ref, wb_ref, nlow_ref, gr_ref, hat_ref, rstd_ref, vec_ref, wo_ref, ctx_ref,
    db_ref, g1_ref, gatt_ref, gctx_ref, dwo_ref, sums_ref,
    nt_sc, acc_sc,
):
    k = pl.program_id(0)
    rows, width = gb_ref.shape
    half = wb_ref.shape[3]
    slots, feat = ctx_ref.shape[0], ctx_ref.shape[2]

    @pl.when(k == 0)
    def _():
        nt_sc[...] = nlow_ref[...].T

    gh = (slope_ref[0] * nn(gb_ref[...], wide(wc_ref))).astype(BF)
    part = nt(gh, wide(wb_ref))

    @pl.when(k == 0)
    def _():
        acc_sc[...] = part

    @pl.when(k > 0)
    def _():
        acc_sc[...] += part

    total = jnp.broadcast_to(jnp.sum(gh.astype(F32), axis=0, keepdims=True), (16, 2 * half))
    total = total.astype(BF)
    grad = nn(nt_sc[...], gh).astype(BF)
    for n in range(2):
        db_ref[n, 0, 0:width] = grad[:, n * half : (n + 1) * half]
        db_ref[n, 0, width : width + 16] = total[:, n * half : (n + 1) * half]

    @pl.when(k == pl.num_programs(0) - 1)
    def _():
        def chunk(n, carry):
            s_gain, s_shift, s_bias = carry
            at = pl.ds(pl.multiple_of(n * ROWS, ROWS), ROWS)
            g = acc_sc[at, :] + gr_ref[at, :]
            hat = hat_ref[at, :]
            s_shift += jnp.sum(g, axis=0, keepdims=True)
            s_gain += jnp.sum(g * hat, axis=0, keepdims=True)
            gh = g * vec_ref[2:3, :]
            g1 = rstd_ref[at, 0:1] * (
                gh
                - jnp.mean(gh, axis=1, keepdims=True)
                - hat * jnp.mean(gh * hat, axis=1, keepdims=True)
            )
            g1_ref[at, :] = g1
            gatt = g1.astype(BF)
            gatt_ref[at, :] = gatt
            s_bias += jnp.sum(gatt.astype(F32), axis=0, keepdims=True)
            for s in range(slots):
                gctx_ref[s, at, :] = nn(gatt, wo_ref[0, s, :, feat : 2 * feat]).astype(BF)
            return s_gain, s_shift, s_bias

        zero = jnp.zeros((1, width), F32)
        s_gain, s_shift, s_bias = lax.fori_loop(0, rows // ROWS, chunk, (zero, zero, zero))
        sums_ref[0:1, :] = s_gain
        sums_ref[1:2, :] = s_shift
        sums_ref[2:3, :] = s_bias
        sums_ref[3:8, :] = jnp.zeros((5, width), F32)
        nt_sc[...] = gatt_ref[...].T
        for s in range(slots):
            dwo_ref[s] = nn(nt_sc[...], ctx_ref[s]).astype(BF)


def ffn_back_call(info, gb, slope, wc, wb, nlow, gr, hat, rstd, vec, wa, ctx):
    slots, rows, feat = ctx.shape
    width = gb.shape[1]
    blocks, half = wb.shape[1], wb.shape[3]
    wblk = lambda r: spec((2, 1, r, half), lambda i, info: (0, i, 0, 0))
    return pl.pallas_call(
        ffn_back_kernel,
        grid_spec=pltpu.PrefetchScalarGridSpec(
            num_scalar_prefetch=1,
            grid=(blocks,),
            in_specs=[
                whole((rows, width)),
                spec((1, rows, 2 * half), lambda i, info: (i, 0, 0)),
                wblk(width),
                wblk(width),
                whole((rows, width)),
                whole((rows, width)),
                whole((rows, width)),
                whole((rows, 128)),
                whole((8, width)),
                spec((1, slots, width, half), lambda i, info: (1 - info[0], 0, 0, 0)),
                whole((slots, rows, feat)),
            ],
            out_specs=[
                wblk(width + 16),
                whole((rows, width)),
                whole((rows, width)),
                whole((slots, rows, feat)),
                whole((slots, width, feat)),
                whole((8, width)),
            ],
            scratch_shapes=[
                pltpu.VMEM((width, rows), BF),
                pltpu.VMEM((rows, width), F32),
            ],
        ),
        out_shape=[
            jax.ShapeDtypeStruct((2, blocks, width + 16, half), BF),
            jax.ShapeDtypeStruct((rows, width), F32),
            jax.ShapeDtypeStruct((rows, width), BF),
            jax.ShapeDtypeStruct((slots, rows, feat), BF),
            jax.ShapeDtypeStruct((slots, width, feat), BF),
            jax.ShapeDtypeStruct((8, width), F32),
        ],
        compiler_params=params(36),
        cost_estimate=cost(12 * rows * width * blocks * half, 3e7),
        name="ffn_back",
    )(info, gb, slope, wc, wb, nlow, gr, hat, rstd, vec, wa, ctx)


def qkv_back_kernel(
    info, x_ref, gq_ref, gkv_ref, gkvo_ref, wa_ref, dwo_ref, g1_ref, one_ref, two_ref,
    da_ref, gx_ref, xt_sc, acc_sc, sums_sc,
):
    s = pl.program_id(0)
    c = info[0]
    width = x_ref.shape[2]
    feat = gq_ref.shape[2]
    edge = slice(width, width + 16)

    @pl.when(s == 0)
    def _():
        xt_sc[...] = x_ref[0].T
        acc_sc[...] = g1_ref[...]
        sums_sc[...] = jnp.zeros_like(sums_sc)
        for n in range(3):
            for m, ref in enumerate((one_ref, two_ref)):
                at = 1 + 2 * (3 * m + n)
                sums_sc[at : at + 1] = ref[n : n + 1, 0 : 2 * feat]
                sums_sc[at + 1 : at + 2] = ref[n : n + 1, 2 * feat : 4 * feat]

    gkv = (gkv_ref[0] + gkvo_ref[0].astype(F32)).astype(BF)
    gq = gq_ref[0]
    da_ref[c, 0, 0:width] = nn(xt_sc[...], gkv).astype(BF)
    da_ref[1 - c, 0, 0:width, 0:feat] = nn(xt_sc[...], gq).astype(BF)
    da_ref[1 - c, 0, 0:width, feat : 2 * feat] = dwo_ref[0]
    sum_q = jnp.sum(gq.astype(F32), axis=0, keepdims=True)
    sum_q = jnp.concatenate((sum_q, jnp.zeros((1, feat), F32)), axis=1)
    sum_kv = jnp.sum(gkv.astype(F32), axis=0, keepdims=True)
    first = lax.broadcasted_iota(jnp.int32, (16, 1), 0) == 0
    da_ref[c, 0, edge] = jnp.where(first, sum_kv, sums_sc[...]).astype(BF)
    da_ref[1 - c, 0, edge] = jnp.where(first, sum_q, sums_sc[...]).astype(BF)
    acc_sc[...] += nt(gkv, wa_ref[c, 0]) + nt(gq, wa_ref[1 - c, 0, :, 0:feat])

    @pl.when(s == pl.num_programs(0) - 1)
    def _():
        gx_ref[...] = acc_sc[...].astype(BF)


def qkv_back_call(info, x, gq, gkv, gkvo, wa, dwo, g1, one, two):
    _, rows, width = x.shape
    slots, _, feat = gq.shape
    half = gkv.shape[2]
    blk = lambda r, w: spec((1, r, w), lambda i, info: (i, 0, 0))
    return pl.pallas_call(
        qkv_back_kernel,
        grid_spec=pltpu.PrefetchScalarGridSpec(
            num_scalar_prefetch=1,
            grid=(slots,),
            in_specs=[
                sequence(rows, width),
                blk(rows, feat),
                blk(rows, half),
                blk(rows, half),
                spec((2, 1, width, half), lambda i, info: (0, i, 0, 0)),
                blk(width, feat),
                whole((rows, width)),
                whole((8, width)),
                whole((8, width)),
            ],
            out_specs=[
                spec((2, 1, width + 16, half), lambda i, info: (0, i, 0, 0)),
                whole((rows, width)),
            ],
            scratch_shapes=[
                pltpu.VMEM((width, rows), BF),
                pltpu.VMEM((rows, width), F32),
                pltpu.VMEM((16, half), F32),
            ],
        ),
        out_shape=[
            jax.ShapeDtypeStruct((2, slots, width + 16, half), BF),
            jax.ShapeDtypeStruct((rows, width), BF),
        ],
        compiler_params=params(24),
        cost_estimate=cost(4 * rows * width * slots * 3 * feat, 2e7),
        name="qkv_back",
    )(info, x, gq, gkv, gkvo, wa, dwo, g1, one, two)


def shards_kernel(info, qkv_ref, out_ref, in_ref, down_ref, a_ref, b_ref, c_ref):
    feat = out_ref.shape[0]
    half = b_ref.shape[1]

    @pl.when(info[0] == 0)
    def _():
        a_ref[:, 0:feat] = qkv_ref[1]
        a_ref[:, feat:] = qkv_ref[2]
        b_ref[...] = in_ref[:, 0:half]
        c_ref[...] = down_ref[0:half, :].T

    @pl.when(info[0] == 1)
    def _():
        a_ref[:, 0:feat] = qkv_ref[0]
        a_ref[:, feat:] = out_ref[...].T
        b_ref[...] = in_ref[:, half:]
        c_ref[...] = down_ref[half:, :].T


def shards_call(info, qkv, out, win, down):
    rows, units = win.shape
    shape = jax.ShapeDtypeStruct((rows, units // 2), BF)
    return pl.pallas_call(
        shards_kernel,
        grid_spec=pltpu.PrefetchScalarGridSpec(
            num_scalar_prefetch=1,
            grid=(1,),
            in_specs=[whole(v.shape) for v in (qkv, out, win, down)],
            out_specs=[whole(shape.shape)] * 3,
        ),
        out_shape=[shape] * 3,
        compiler_params=params(8),
        cost_estimate=cost(0, 2e6),
        name="shards",
    )(info, qkv, out, win, down)


def wide_owned_kernel(info, own_ref, other_ref, in_ref, down_ref, din_ref):
    shard, units = in_ref.shape
    half = units // 2

    def write(first, second):
        for n, ref in enumerate((first, second)):
            cols = slice(n * half, (n + 1) * half)
            in_ref[:, cols] = ref[0:shard, :].astype(F32)
            din_ref[:, cols] = ref[shard : shard + 1, :].astype(F32)
            down_ref[cols, :] = ref[shard + 16 : 2 * shard + 16, :].astype(F32).T

    @pl.when(info[0] == 0)
    def _():
        write(own_ref, other_ref)

    @pl.when(info[0] == 1)
    def _():
        write(other_ref, own_ref)


def wide_owned_call(info, own, other):
    total, half = own.shape
    shard = (total - 16) // 2
    shapes = [(shard, 2 * half), (2 * half, shard), (1, 2 * half)]
    return pl.pallas_call(
        wide_owned_kernel,
        grid_spec=pltpu.PrefetchScalarGridSpec(
            num_scalar_prefetch=1,
            grid=(1,),
            in_specs=[whole((total, half))] * 2,
            out_specs=[whole(v) for v in shapes],
        ),
        out_shape=[jax.ShapeDtypeStruct(v, F32) for v in shapes],
        compiler_params=params(8),
        cost_estimate=cost(0, 2e6),
        name="wide_owned",
    )(info, own, other)


def owned_kernel(info, own_ref, other_ref, qkv_ref, out_ref, bias_ref, sums_ref):
    feat = out_ref.shape[0]
    shard = out_ref.shape[1]
    half = 2 * feat

    def write(first, second):
        qkv_ref[0] = second[0:shard, 0:feat].astype(F32)
        qkv_ref[1] = first[0:shard, 0:feat].astype(F32)
        qkv_ref[2] = first[0:shard, feat:].astype(F32)
        out_ref[...] = second[0:shard, feat:].astype(F32).T
        bias_ref[0:1, :] = second[shard : shard + 1, 0:feat].astype(F32)
        bias_ref[1:2, :] = first[shard : shard + 1, feat:].astype(F32)

    @pl.when(info[0] == 0)
    def _():
        write(own_ref, other_ref)

    @pl.when(info[0] == 1)
    def _():
        write(other_ref, own_ref)

    for n in range(6):
        at = shard + 1 + 2 * n
        sums_ref[n : n + 1, 0:half] = own_ref[at : at + 1, :].astype(F32)
        sums_ref[n : n + 1, half:] = own_ref[at + 1 : at + 2, :].astype(F32)


def owned_call(info, own, other):
    total, half = own.shape
    shard, feat = total - 16, half // 2
    shapes = [(3, shard, feat), (feat, shard), (2, feat), (6, 2 * half)]
    return pl.pallas_call(
        owned_kernel,
        grid_spec=pltpu.PrefetchScalarGridSpec(
            num_scalar_prefetch=1,
            grid=(1,),
            in_specs=[whole((total, half))] * 2,
            out_specs=[whole(v) for v in shapes],
        ),
        out_shape=[jax.ShapeDtypeStruct(v, F32) for v in shapes],
        compiler_params=params(8),
        cost_estimate=cost(0, 2e6),
        name="owned",
    )(info, own, other)


def ring(size, step):
    return [(i, (i + step) % size) for i in range(size)]


def tie(*values):
    return lax.optimization_barrier(values)


def swap(value):
    return lax.ppermute(value, "ctx", C_SWAP)


def by_x(value):
    return lax.ppermute(value, "tp", X_SWAP)


def by_y(value):
    return lax.ppermute(value, "tp", Y_SWAP)


def column_gather(shard, rank, size):
    if size > 4:
        return lax.all_gather(shard, "fsdp", axis=0, tiled=True)
    rows = shard.shape[0]
    full = jnp.zeros((size * rows,) + shard.shape[1:], shard.dtype)
    full = lax.dynamic_update_slice_in_dim(full, shard, rank * rows, 0)
    for step in range(1, size):
        got = lax.ppermute(shard, "fsdp", ring(size, step))
        full = lax.dynamic_update_slice_in_dim(full, got, ((rank - step) % size) * rows, 0)
    return full


def ring_sum(piece, rank, size):
    got = [piece(rank).astype(F32)]
    for step in range(1, size):
        got.append(lax.ppermute(piece((rank + step) % size), "fsdp", ring(size, step)).astype(F32))
    while len(got) > 1:
        cut = len(got) // 2
        got = [a + b for a, b in zip(got[:cut], got[cut:], strict=True)]
    return got[0].astype(BF)


def column_scatter(full, width, rank, size):
    rows = width // size
    extra = full[width:]
    if size > 4:
        own = lax.psum_scatter(full[:width], "fsdp", scatter_dimension=0, tiled=True)
        return jnp.concatenate((own, lax.psum(extra, "fsdp")), axis=0)

    def piece(owner):
        return jnp.concatenate(
            (lax.dynamic_slice_in_dim(full, owner * rows, rows, 0), extra), axis=0
        )

    return ring_sum(piece, rank, size)


def column_scatter_first(blocks, rank, size):
    if size > 4:
        return lax.psum_scatter(blocks, "fsdp", scatter_dimension=1, tiled=True)
    rows = blocks.shape[1] // size
    return ring_sum(lambda owner: lax.dynamic_slice_in_dim(blocks, owner * rows, rows, 1), rank, size)


def plane_second(from_x, from_y):
    cut = from_x.shape[0] // 2
    return by_x(from_y[:cut]), by_y(from_x[cut:])


def add(a, b):
    return (a.astype(F32) + b.astype(F32)).astype(BF)


def scatter_first(blocks):
    cut = 384 if blocks.shape[1] > 384 else blocks.shape[1] // 2
    up, down = blocks[:, :cut], blocks[:, cut:]
    return up, down, by_x(jnp.stack((up[1], up[3]))), by_y(jnp.stack((down[2], down[3])))


def scatter_second(up, down, got_up, got_down):
    from_up = by_y(add(up[2], got_up[1]))
    from_down = by_x(add(down[1], got_down[1]))
    return add(up[0], got_up[0]), add(down[0], got_down[0]), from_up, from_down


def scatter_done(mid_up, mid_down, from_up, from_down):
    return jnp.concatenate((add(mid_up, from_up), add(mid_down, from_down)), axis=0)


def place_sequences(slots, index, dtype):
    out = jnp.zeros((len(slots),) + slots[0].shape, dtype)
    for distance, block in enumerate(slots):
        out = lax.dynamic_update_slice(out, block.astype(dtype)[None], (index ^ distance, 0, 0))
    return out


def per_device(
    tokens, lengths, qkv_weight, qv_bias, out_weight, out_bias, ffn_in, ffn_in_bias,
    ffn_out, ffn_out_bias, norm_gains, norm_shifts, cotangent,
):
    size = lax.axis_size("fsdp")
    rank = lax.axis_index("fsdp")
    c = lax.axis_index("ctx")
    t = lax.axis_index("tp")
    seqs, rows, width = tokens.shape
    assert lax.axis_size("tp") == 4 and lax.axis_size("ctx") == 2 and seqs == 4
    feat = qkv_weight.shape[2]
    units = ffn_in.shape[1]
    half = units // 2
    assert half == 2 * feat
    length = lax.dynamic_index_in_dim(lengths, t, 0, keepdims=False)
    info = jnp.stack((c.astype(jnp.int32), length, t.astype(jnp.int32)))

    shard_a, shard_b, shard_c = shards_call(info, qkv_weight, out_weight, ffn_in, ffn_out)

    bias_own = jnp.concatenate((qv_bias.reshape(-1), ffn_in_bias)).reshape(1, -1)
    bias_x = by_x(bias_own)
    bias_y = by_y(bias_own)
    bias_x, shard_a = tie(bias_x, shard_a)
    bias_d = by_y(bias_x)
    col_a = column_gather(shard_a, rank, size)
    col_a, shard_b, bias_y, bias_d = tie(col_a, shard_b, bias_y, bias_d)
    ax, ay = by_x(col_a), by_y(col_a)
    col_b = column_gather(shard_b, rank, size)
    ax, ay = tie(ax, ay)
    au, al = plane_second(ax, ay)
    three = jnp.stack((col_a, ax, ay))
    three_other = swap(three)
    au, al, col_b, shard_c = tie(au, al, col_b, shard_c)
    last = jnp.concatenate((au, al), axis=0)[None]
    last_other = swap(last)
    bx, by = by_x(col_b), by_y(col_b)
    col_c = column_gather(shard_c, rank, size)
    wa = jnp.concatenate((three, last, three_other, last_other), axis=0)
    wa = wa.reshape(2, 4, width, half)

    bias = jnp.stack((bias_own, bias_x, bias_y, bias_d))
    q_bias = bias[:, :, :feat]
    kv_bias = jnp.concatenate((jnp.zeros_like(q_bias), bias[:, :, feat : 2 * feat]), axis=2)
    in_bias = bias[:, :, 2 * feat :]
    swapped = jnp.concatenate((in_bias[:, :, half:], in_bias[:, :, :half]), axis=2)
    in_bias = jnp.where(c == 0, in_bias, swapped)
    zero_row = jnp.zeros_like(out_bias)
    vec = jnp.stack((out_bias, ffn_out_bias, norm_gains[0], norm_gains[1], norm_shifts[0], norm_shifts[1], zero_row, zero_row))

    q, kv = qkv_call(info, tokens, wa, q_bias, kv_bias)
    q, kv, bx, by, col_c = tie(q, kv, bx, by, col_c)
    kv_other = swap(kv)
    bu, bl = plane_second(bx, by)
    three_b = jnp.stack((col_b, bx, by))
    three_b_other = swap(three_b)
    cx, cy = by_x(col_c), by_y(col_c)
    context, lse = attn_call(info, q, kv, kv_other)
    context, lse, bu, bl, three_b_other, cx, cy = tie(context, lse, bu, bl, three_b_other, cx, cy)
    cu, cl = plane_second(cx, cy)
    last_b = jnp.concatenate((bu, bl), axis=0)[None]
    three_c = jnp.stack((col_c, cx, cy))
    three_c_other = swap(three_c)
    wb = jnp.concatenate((three_b, last_b, three_b_other, swap(last_b)), axis=0)
    wb = wb.reshape(2, 4, width, half)
    last_c = jnp.concatenate((cu, cl), axis=0)[None]
    wc = jnp.concatenate((three_c, last_c, three_c_other, swap(last_c)), axis=0)
    wc = wc.reshape(2, 4, width, half)

    act, slope, nlow, hat, rstd, out, g_branch, g_r2, sums_two = ffn_call(
        info, context, wa, tokens, cotangent, vec, in_bias, wb, wc
    )
    out_x, out_y = by_x(out), by_y(out)
    dc = down_call(info, g_branch, act)
    dc, g_branch = tie(dc, g_branch)
    dc_got = swap(dc[1])
    db, g_r1, g_att, g_context, dwo, sums_one = ffn_back_call(
        info, g_branch, slope, wc, wb, nlow, g_r2, hat, rstd, vec, wa, context
    )
    db, g_context, dc_got, out_x, out_y = tie(db, g_context, dc_got, out_x, out_y)
    out_u, out_l = plane_second(out_x, out_y)
    row_c = column_scatter_first(add(dc[0], dc_got), rank, size)
    db_got = swap(db[1])
    gq1, gkv1, gkv_send1 = attn_back_call(info, q, kv, kv_other, lse, context, g_context, 0, 2)
    gq1, gkv1, gkv_send1, q, db_got, out_u, out_l = tie(
        gq1, gkv1, gkv_send1, q, db_got, out_u, out_l
    )
    part_b = scatter_first(add(db[0], db_got))
    gkv_got1 = swap(gkv_send1)
    gq2, gkv2, gkv_send2 = attn_back_call(info, q, kv, kv_other, lse, context, g_context, 2, 2)
    gq2, gkv2, gkv_send2, gkv_got1, row_c, *part_b = tie(
        gq2, gkv2, gkv_send2, gkv_got1, row_c, *part_b
    )
    part_b = scatter_second(*part_b)
    part_c = scatter_first(row_c)
    gkv_got2 = swap(gkv_send2)
    gq = jnp.concatenate((gq1, gq2), axis=0)
    gkv = jnp.concatenate((gkv1, gkv2), axis=0)
    gkv_got = jnp.concatenate((gkv_got1, gkv_got2), axis=0)
    da, g_tokens = qkv_back_call(
        info, tokens, gq, gkv, gkv_got, wa, dwo, g_r1, sums_one, sums_two
    )
    da, g_tokens, *parts = tie(da, g_tokens, *part_b, *part_c)
    part_b, part_c = parts[:4], parts[4:]
    da_got = swap(da[1])
    gt_x, gt_y = by_x(g_tokens), by_y(g_tokens)
    own_b = column_scatter(scatter_done(*part_b), width, rank, size)
    own_c = scatter_done(*scatter_second(*part_c))
    part_a = scatter_first(add(da[0], da_got))
    gt_x, gt_y, own_b, own_c = tie(gt_x, gt_y, own_b, own_c)
    gt_u, gt_l = plane_second(gt_x, gt_y)
    own_bc = jnp.concatenate((own_b, own_c), axis=0)
    other_bc = swap(own_bc)
    part_a = tie(*part_a)
    own_a = column_scatter(scatter_done(*scatter_second(*part_a)), width, rank, size)
    layer_output = place_sequences((out, out_x, out_y, jnp.concatenate((out_u, out_l), axis=0)), t, BF)
    grad_tokens = place_sequences(
        (g_tokens, gt_x, gt_y, jnp.concatenate((gt_u, gt_l), axis=0)), t, F32
    )
    grad_in, grad_down, d_in = wide_owned_call(info, own_bc, other_bc)
    grad_qkv, grad_out, d_qv, sums = owned_call(info, own_a, swap(own_a))
    return (
        layer_output,
        grad_tokens,
        grad_qkv,
        d_qv,
        grad_out,
        sums[2],
        grad_in,
        d_in[0],
        grad_down,
        sums[5],
        jnp.stack((sums[0], sums[3])),
        jnp.stack((sums[1], sums[4])),
    )


def solution(mesh):
    placed = (
        P("fsdp", "ctx", None),
        P("fsdp"),
        P(None, "fsdp", "tp"),
        P(None, "tp"),
        P("tp", "fsdp"),
        P(),
        P("fsdp", "tp"),
        P("tp"),
        P("tp", "fsdp"),
        P(),
        P(),
        P(),
        P("fsdp", "ctx", None),
    )
    return jax.shard_map(
        per_device,
        mesh=mesh,
        in_specs=placed,
        out_specs=(
            P("fsdp", "ctx", None),
            P("fsdp", "ctx", None),
            P(None, "fsdp", "tp"),
            P(None, "tp"),
            P("tp", "fsdp"),
            P(),
            P("fsdp", "tp"),
            P("tp"),
            P("tp", "fsdp"),
            P(),
            P(),
            P(),
        ),
        check_vma=False,
    )
```

```python
import functools
import math

import jax
import jax.numpy as jnp
from jax import lax
from jax.experimental import pallas as pl
from jax.experimental.pallas import tpu as pltpu
from jax.sharding import PartitionSpec as P

HD = 64
EPS = 1e-05
MASKED = -1000000000.0
LOG2E = math.log2(math.e)
SCALE = 0.125
BF = jnp.bfloat16
F32 = jnp.float32
MIB = 1024 * 1024

X_SWAP = [(0, 1), (1, 0), (2, 3), (3, 2)]
Y_SWAP = [(0, 2), (2, 0), (1, 3), (3, 1)]
C_SWAP = [(0, 1), (1, 0)]


def nn(a, b):
    return lax.dot_general(a, b, (((1,), (0,)), ((), ())), preferred_element_type=F32)


def nt(a, b):
    return lax.dot_general(a, b, (((1,), (1,)), ((), ())), preferred_element_type=F32)


def tn(a, b):
    return lax.dot_general(a, b, (((0,), (0,)), ((), ())), preferred_element_type=F32)


def params(mib):
    return pltpu.CompilerParams(
        dimension_semantics=("arbitrary",), vmem_limit_bytes=mib * MIB
    )


def cost(flops, moved, trans=0):
    return pl.CostEstimate(flops=int(flops), bytes_accessed=int(moved), transcendentals=int(trans))


def spec(shape, index):
    return pl.BlockSpec(shape, index)


def sequence(rows, width):
    return pl.BlockSpec((1, rows, width), lambda i, info: (info[2], 0, 0))


def whole(shape):
    zeros = (0,) * len(shape)
    return pl.BlockSpec(shape, lambda i, info: zeros)


def qkv_kernel(info, x_ref, a_ref, qb_ref, kvb_ref, q_ref, kv_ref):
    c = info[0]
    x = x_ref[0]
    kv_ref[0] = (nn(x, a_ref[c, 0]) + kvb_ref[0]).astype(BF)
    q_ref[0] = (nn(x, a_ref[1 - c, 0, :, 0 : q_ref.shape[2]]) + qb_ref[0]).astype(BF)


def qkv_call(info, x, wa, qb, kvb):
    _, rows, width = x.shape
    slots, half = wa.shape[1], wa.shape[3]
    feat = half // 2
    return pl.pallas_call(
        qkv_kernel,
        grid_spec=pltpu.PrefetchScalarGridSpec(
            num_scalar_prefetch=1,
            grid=(slots,),
            in_specs=[
                sequence(rows, width),
                spec((2, 1, width, half), lambda i, info: (0, i, 0, 0)),
                spec((1, 1, feat), lambda i, info: (i, 0, 0)),
                spec((1, 1, half), lambda i, info: (i, 0, 0)),
            ],
            out_specs=[
                spec((1, rows, feat), lambda i, info: (i, 0, 0)),
                spec((1, rows, half), lambda i, info: (i, 0, 0)),
            ],
        ),
        out_shape=[
            jax.ShapeDtypeStruct((slots, rows, feat), BF),
            jax.ShapeDtypeStruct((slots, rows, half), BF),
        ],
        compiler_params=params(12),
        cost_estimate=cost(2 * rows * width * slots * 3 * feat, 8e6),
        name="qkv",
    )(info, x, wa, qb, kvb)


def key_bias(info, rows, mine):
    owner = info[0] if mine else 1 - info[0]
    position = owner * rows + lax.broadcasted_iota(jnp.int32, (1, rows), 1)
    return jnp.where(position < info[1], 0.0, MASKED)


def attn_kernel(info, q_ref, kv_ref, kvo_ref, ctx_ref, lse_ref):
    rows, feat = q_ref.shape[1], q_ref.shape[2]
    bias_m, bias_o = key_bias(info, rows, True), key_bias(info, rows, False)
    lane = lax.broadcasted_iota(jnp.int32, (1, 128), 1)
    lse_all = jnp.zeros((rows, 128), F32)
    for h in range(feat // HD):
        cols = slice(h * HD, (h + 1) * HD)
        vcols = slice(feat + h * HD, feat + (h + 1) * HD)
        q = q_ref[0, :, cols]
        s_m = nt(q, kv_ref[0, :, cols]) * (SCALE * LOG2E) + bias_m
        s_o = nt(q, kvo_ref[0, :, cols]) * (SCALE * LOG2E) + bias_o
        top = jnp.maximum(
            jnp.max(s_m, axis=1, keepdims=True), jnp.max(s_o, axis=1, keepdims=True)
        )
        e_m = jnp.exp2(s_m - top)
        e_o = jnp.exp2(s_o - top)
        total = jnp.sum(e_m, axis=1, keepdims=True) + jnp.sum(e_o, axis=1, keepdims=True)
        out = nn(e_m.astype(BF), kv_ref[0, :, vcols]) + nn(e_o.astype(BF), kvo_ref[0, :, vcols])
        ctx_ref[0, :, cols] = (out * (1.0 / total)).astype(BF)
        lse_all = jnp.where(lane == h, top + jnp.log2(total), lse_all)
    lse_ref[0] = lse_all


def attn_call(info, q, kv, kvo):
    slots, rows, feat = q.shape
    half = kv.shape[2]
    blk = lambda w: spec((1, rows, w), lambda i, info: (i, 0, 0))
    heads = slots * feat // HD
    return pl.pallas_call(
        attn_kernel,
        grid_spec=pltpu.PrefetchScalarGridSpec(
            num_scalar_prefetch=1,
            grid=(slots,),
            in_specs=[blk(feat), blk(half), blk(half)],
            out_specs=[blk(feat), blk(128)],
        ),
        out_shape=[
            jax.ShapeDtypeStruct((slots, rows, feat), BF),
            jax.ShapeDtypeStruct((slots, rows, 128), F32),
        ],
        compiler_params=params(24),
        cost_estimate=cost(16 * rows * rows * 2 * HD * heads, 8e6, 2 * rows * rows * heads),
        name="attn",
    )(info, q, kv, kvo)


def attn_back_kernel(
    info, q_ref, kv_ref, kvo_ref, lse_ref, ctx_ref, g_ref, gq_ref, gkv_ref, gkvo_ref
):
    rows, feat = q_ref.shape[1], q_ref.shape[2]
    bias_m, bias_o = key_bias(info, rows, True), key_bias(info, rows, False)
    lane = lax.broadcasted_iota(jnp.int32, (1, 128), 1)
    lse_all = lse_ref[0]
    for h in range(feat // HD):
        cols = slice(h * HD, (h + 1) * HD)
        vcols = slice(feat + h * HD, feat + (h + 1) * HD)
        q, g = q_ref[0, :, cols], g_ref[0, :, cols]
        k_m, k_o = kv_ref[0, :, cols], kvo_ref[0, :, cols]
        lse = jnp.sum(jnp.where(lane == h, lse_all, 0.0), axis=1, keepdims=True)
        inner = jnp.sum(g.astype(F32) * ctx_ref[0, :, cols].astype(F32), axis=1, keepdims=True)
        p_m = jnp.exp2(nt(q, k_m) * (SCALE * LOG2E) + bias_m - lse)
        p_o = jnp.exp2(nt(q, k_o) * (SCALE * LOG2E) + bias_o - lse)
        gs_m = (p_m * (nt(g, kv_ref[0, :, vcols]) - inner)).astype(BF)
        gs_o = (p_o * (nt(g, kvo_ref[0, :, vcols]) - inner)).astype(BF)
        g_t, q_t = g.T, q.T
        gkv_ref[0, :, vcols] = nn(g_t, p_m.astype(BF)).T
        gkvo_ref[0, :, vcols] = nn(g_t, p_o.astype(BF)).T.astype(BF)
        gkv_ref[0, :, cols] = nn(q_t, gs_m).T * SCALE
        gkvo_ref[0, :, cols] = (nn(q_t, gs_o).T * SCALE).astype(BF)
        gq_ref[0, :, cols] = ((nn(gs_m, k_m) + nn(gs_o, k_o)) * SCALE).astype(BF)


def attn_back_call(info, q, kv, kvo, lse, ctx, g, first, slots):
    _, rows, feat = q.shape
    half = kv.shape[2]
    src = lambda w: spec((1, rows, w), lambda i, info: (i + first, 0, 0))
    blk = lambda w: spec((1, rows, w), lambda i, info: (i, 0, 0))
    heads = slots * feat // HD
    return pl.pallas_call(
        attn_back_kernel,
        grid_spec=pltpu.PrefetchScalarGridSpec(
            num_scalar_prefetch=1,
            grid=(slots,),
            in_specs=[src(feat), src(half), src(half), src(128), src(feat), src(feat)],
            out_specs=[blk(feat), blk(half), blk(half)],
        ),
        out_shape=[
            jax.ShapeDtypeStruct((slots, rows, feat), BF),
            jax.ShapeDtypeStruct((slots, rows, half), F32),
            jax.ShapeDtypeStruct((slots, rows, half), BF),
        ],
        compiler_params=params(24),
        cost_estimate=cost(40 * rows * rows * 2 * HD * heads, 12e6, 2 * rows * rows * heads),
        name="attn_back",
    )(info, q, kv, kvo, lse, ctx, g)


ROWS = 256


def wide(ref):
    return jnp.concatenate((ref[0, 0], ref[1, 0]), axis=1)


def gathered(own, other):
    join = lambda ref: ref[:, 0].reshape(ref.shape[0] * ref.shape[2], ref.shape[3])
    return jnp.concatenate((join(own), join(other)), axis=1)


def gathered_spec(array):
    pieces, _, rows, half = array.shape
    return pl.BlockSpec((pieces, 1, rows, half), lambda i, info: (0, info[2] ^ i, 0, 0))


def row_mask(info, rows, start, count):
    position = info[0] * rows + start + lax.broadcasted_iota(jnp.int32, (count, 1), 0)
    return (position < info[1]).astype(F32)


def ffn_kernel(
    info, ctx_ref, wo_ref, x_ref, cot_ref, vec_ref, bin_ref, wb_ref, wc_ref, wco_ref,
    act_ref, slope_ref, nlow_ref, hat_ref, rstd_ref, out_ref, gb_ref, gr_ref, sums_ref,
    normed_sc, branch_sc,
):
    k = pl.program_id(0)
    _, rows, width = x_ref.shape
    slots, feat = ctx_ref.shape[0], ctx_ref.shape[2]

    @pl.when(k == 0)
    def _():
        def chunk(n, carry):
            at = pl.ds(pl.multiple_of(n * ROWS, ROWS), ROWS)
            res = x_ref[0, at, :].astype(F32) + vec_ref[0:1, :]
            for s in range(slots):
                res += nt(ctx_ref[s, at, :], wo_ref[0, s, :, feat : 2 * feat])
            center = jnp.mean(res, axis=1, keepdims=True)
            res = res - center
            rstd = lax.rsqrt(jnp.mean(res * res, axis=1, keepdims=True) + EPS)
            hat = res * rstd
            normed = hat * vec_ref[2:3, :] + vec_ref[4:5, :]
            hat_ref[at, :] = hat
            rstd_ref[at, :] = jnp.broadcast_to(rstd, (ROWS, 128))
            normed_sc[at, :] = normed
            nlow_ref[at, :] = normed.astype(BF)
            return carry

        lax.fori_loop(0, rows // ROWS, chunk, 0)

    u = nn(nlow_ref[...], wide(wb_ref)) + bin_ref[0]
    cdf = 0.5 + 0.5 * lax.erf(u * math.sqrt(0.5))
    act = (u * cdf).astype(BF)
    act_ref[0] = act
    slope_ref[0] = cdf + u * (jnp.exp(u * u * -0.5) * (1.0 / math.sqrt(2.0 * math.pi)))
    part = nt(act, gathered(wc_ref, wco_ref))

    @pl.when(k == 0)
    def _():
        branch_sc[...] = part

    @pl.when(k > 0)
    def _():
        branch_sc[...] += part

    @pl.when(k == pl.num_programs(0) - 1)
    def _():
        def chunk(n, carry):
            s_gain, s_shift, s_bias = carry
            at = pl.ds(pl.multiple_of(n * ROWS, ROWS), ROWS)
            res = normed_sc[at, :] + branch_sc[at, :] + vec_ref[1:2, :]
            center = jnp.mean(res, axis=1, keepdims=True)
            res = res - center
            rstd = lax.rsqrt(jnp.mean(res * res, axis=1, keepdims=True) + EPS)
            hat = res * rstd
            out_ref[at, :] = (hat * vec_ref[3:4, :] + vec_ref[5:6, :]).astype(BF)
            g = cot_ref[0, at, :].astype(F32) * row_mask(info, rows, n * ROWS, ROWS)
            s_shift += jnp.sum(g, axis=0, keepdims=True)
            s_gain += jnp.sum(g * hat, axis=0, keepdims=True)
            gh = g * vec_ref[3:4, :]
            gr = rstd * (
                gh
                - jnp.mean(gh, axis=1, keepdims=True)
                - hat * jnp.mean(gh * hat, axis=1, keepdims=True)
            )
            gr_ref[at, :] = gr
            gb = gr.astype(BF)
            gb_ref[at, :] = gb
            s_bias += jnp.sum(gb.astype(F32), axis=0, keepdims=True)
            return s_gain, s_shift, s_bias

        zero = jnp.zeros((1, width), F32)
        s_gain, s_shift, s_bias = lax.fori_loop(0, rows // ROWS, chunk, (zero, zero, zero))
        sums_ref[0:1, :] = s_gain
        sums_ref[1:2, :] = s_shift
        sums_ref[2:3, :] = s_bias
        sums_ref[3:8, :] = jnp.zeros((5, width), F32)


def ffn_call(info, ctx, wa, x, cot, vec, b_in, wb, wc, wco):
    slots, rows, feat = ctx.shape
    width = x.shape[2]
    blocks, half = wb.shape[1], wb.shape[3]
    units = 2 * half
    kblk = lambda r, w: spec((1, r, w), lambda i, info: (i, 0, 0))
    wblk = spec((2, 1, width, half), lambda i, info: (0, i, 0, 0))
    return pl.pallas_call(
        ffn_kernel,
        grid_spec=pltpu.PrefetchScalarGridSpec(
            num_scalar_prefetch=1,
            grid=(blocks,),
            in_specs=[
                whole((slots, rows, feat)),
                spec((1, slots, width, half), lambda i, info: (1 - info[0], 0, 0, 0)),
                sequence(rows, width),
                sequence(rows, width),
                whole((8, width)),
                kblk(1, units),
                wblk,
                gathered_spec(wc),
                gathered_spec(wco),
            ],
            out_specs=[
                kblk(rows, units),
                kblk(rows, units),
                whole((rows, width)),
                whole((rows, width)),
                whole((rows, 128)),
                whole((rows, width)),
                whole((rows, width)),
                whole((rows, width)),
                whole((8, width)),
            ],
            scratch_shapes=[pltpu.VMEM((rows, width), F32), pltpu.VMEM((rows, width), F32)],
        ),
        out_shape=[
            jax.ShapeDtypeStruct((blocks, rows, units), BF),
            jax.ShapeDtypeStruct((blocks, rows, units), F32),
            jax.ShapeDtypeStruct((rows, width), BF),
            jax.ShapeDtypeStruct((rows, width), F32),
            jax.ShapeDtypeStruct((rows, 128), F32),
            jax.ShapeDtypeStruct((rows, width), BF),
            jax.ShapeDtypeStruct((rows, width), BF),
            jax.ShapeDtypeStruct((rows, width), F32),
            jax.ShapeDtypeStruct((8, width), F32),
        ],
        compiler_params=params(28),
        cost_estimate=cost(12 * rows * width * blocks * units, 3e7, 2 * rows * blocks * units),
        name="ffn",
    )(info, ctx, wa, x, cot, vec, b_in, wb, wc, wco)


def down_kernel(info, gb_ref, act_ref, dc_ref, gt_sc):
    @pl.when(pl.program_id(0) == 0)
    def _():
        gt_sc[...] = gb_ref[...].T

    grad = nn(gt_sc[...], act_ref[0]).astype(BF)
    pieces, _, _, rows, half = dc_ref.shape
    c = info[0]
    for n in range(pieces):
        dc_ref[n, c, 0] = grad[n * rows : (n + 1) * rows, :half]
        dc_ref[n, 1 - c, 0] = grad[n * rows : (n + 1) * rows, half:]


def down_call(info, gb, act, pieces):
    rows, width = gb.shape
    blocks, _, units = act.shape
    shape = (pieces, 2, blocks, width // pieces, units // 2)
    return pl.pallas_call(
        down_kernel,
        grid_spec=pltpu.PrefetchScalarGridSpec(
            num_scalar_prefetch=1,
            grid=(blocks,),
            in_specs=[whole((rows, width)), spec((1, rows, units), lambda i, info: (i, 0, 0))],
            out_specs=spec(
                shape[:2] + (1,) + shape[3:], lambda i, info: (0, 0, info[2] ^ i, 0, 0)
            ),
            scratch_shapes=[pltpu.VMEM((width, rows), BF)],
        ),
        out_shape=jax.ShapeDtypeStruct(shape, BF),
        compiler_params=params(16),
        cost_estimate=cost(2 * rows * width * blocks * units, 9e6),
        name="down_grad",
    )(info, gb, act)


def ffn_back_kernel(
    info, gb_ref, slope_ref, wc_ref, wco_ref, wb_ref, nlow_ref, gr_ref, hat_ref, rstd_ref, vec_ref, wo_ref, ctx_ref,
    db_ref, g1_ref, gatt_ref, gctx_ref, dwo_ref, sums_ref,
    nt_sc, acc_sc,
):
    k = pl.program_id(0)
    rows, width = gb_ref.shape
    half = wb_ref.shape[3]
    slots, feat = ctx_ref.shape[0], ctx_ref.shape[2]

    @pl.when(k == 0)
    def _():
        nt_sc[...] = nlow_ref[...].T

    gh = (slope_ref[0] * nn(gb_ref[...], gathered(wc_ref, wco_ref))).astype(BF)
    part = nt(gh, wide(wb_ref))

    @pl.when(k == 0)
    def _():
        acc_sc[...] = part

    @pl.when(k > 0)
    def _():
        acc_sc[...] += part

    total = jnp.broadcast_to(jnp.sum(gh.astype(F32), axis=0, keepdims=True), (16, 2 * half))
    total = total.astype(BF)
    grad = nn(nt_sc[...], gh).astype(BF)
    for n in range(2):
        db_ref[n, 0, 0:width] = grad[:, n * half : (n + 1) * half]
        db_ref[n, 0, width : width + 16] = total[:, n * half : (n + 1) * half]

    @pl.when(k == pl.num_programs(0) - 1)
    def _():
        def chunk(n, carry):
            s_gain, s_shift, s_bias = carry
            at = pl.ds(pl.multiple_of(n * ROWS, ROWS), ROWS)
            g = acc_sc[at, :] + gr_ref[at, :]
            hat = hat_ref[at, :]
            s_shift += jnp.sum(g, axis=0, keepdims=True)
            s_gain += jnp.sum(g * hat, axis=0, keepdims=True)
            gh = g * vec_ref[2:3, :]
            g1 = rstd_ref[at, 0:1] * (
                gh
                - jnp.mean(gh, axis=1, keepdims=True)
                - hat * jnp.mean(gh * hat, axis=1, keepdims=True)
            )
            g1_ref[at, :] = g1
            gatt = g1.astype(BF)
            gatt_ref[at, :] = gatt
            s_bias += jnp.sum(gatt.astype(F32), axis=0, keepdims=True)
            for s in range(slots):
                gctx_ref[s, at, :] = nn(gatt, wo_ref[0, s, :, feat : 2 * feat]).astype(BF)
            return s_gain, s_shift, s_bias

        zero = jnp.zeros((1, width), F32)
        s_gain, s_shift, s_bias = lax.fori_loop(0, rows // ROWS, chunk, (zero, zero, zero))
        sums_ref[0:1, :] = s_gain
        sums_ref[1:2, :] = s_shift
        sums_ref[2:3, :] = s_bias
        sums_ref[3:8, :] = jnp.zeros((5, width), F32)
        nt_sc[...] = gatt_ref[...].T
        for s in range(slots):
            dwo_ref[s] = nn(nt_sc[...], ctx_ref[s]).astype(BF)


def ffn_back_call(info, gb, slope, wc, wco, wb, nlow, gr, hat, rstd, vec, wa, ctx):
    slots, rows, feat = ctx.shape
    width = gb.shape[1]
    blocks, half = wb.shape[1], wb.shape[3]
    wblk = lambda r: spec((2, 1, r, half), lambda i, info: (0, i, 0, 0))
    return pl.pallas_call(
        ffn_back_kernel,
        grid_spec=pltpu.PrefetchScalarGridSpec(
            num_scalar_prefetch=1,
            grid=(blocks,),
            in_specs=[
                whole((rows, width)),
                spec((1, rows, 2 * half), lambda i, info: (i, 0, 0)),
                gathered_spec(wc),
                gathered_spec(wco),
                wblk(width),
                whole((rows, width)),
                whole((rows, width)),
                whole((rows, width)),
                whole((rows, 128)),
                whole((8, width)),
                spec((1, slots, width, half), lambda i, info: (1 - info[0], 0, 0, 0)),
                whole((slots, rows, feat)),
            ],
            out_specs=[
                wblk(width + 16),
                whole((rows, width)),
                whole((rows, width)),
                whole((slots, rows, feat)),
                whole((slots, width, feat)),
                whole((8, width)),
            ],
            scratch_shapes=[
                pltpu.VMEM((width, rows), BF),
                pltpu.VMEM((rows, width), F32),
            ],
        ),
        out_shape=[
            jax.ShapeDtypeStruct((2, blocks, width + 16, half), BF),
            jax.ShapeDtypeStruct((rows, width), F32),
            jax.ShapeDtypeStruct((rows, width), BF),
            jax.ShapeDtypeStruct((slots, rows, feat), BF),
            jax.ShapeDtypeStruct((slots, width, feat), BF),
            jax.ShapeDtypeStruct((8, width), F32),
        ],
        compiler_params=params(36),
        cost_estimate=cost(12 * rows * width * blocks * half, 3e7),
        name="ffn_back",
    )(info, gb, slope, wc, wco, wb, nlow, gr, hat, rstd, vec, wa, ctx)


def qkv_back_kernel(
    info, x_ref, gq_ref, gkv_ref, gkvo_ref, wa_ref, dwo_ref, g1_ref, one_ref, two_ref,
    da_ref, gx_ref, xt_sc, acc_sc, sums_sc,
):
    s = pl.program_id(0)
    c = info[0]
    width = x_ref.shape[2]
    feat = gq_ref.shape[2]
    edge = slice(width, width + 16)

    @pl.when(s == 0)
    def _():
        xt_sc[...] = x_ref[0].T
        acc_sc[...] = g1_ref[...]
        sums_sc[...] = jnp.zeros_like(sums_sc)
        for n in range(3):
            for m, ref in enumerate((one_ref, two_ref)):
                at = 1 + 2 * (3 * m + n)
                sums_sc[at : at + 1] = ref[n : n + 1, 0 : 2 * feat]
                sums_sc[at + 1 : at + 2] = ref[n : n + 1, 2 * feat : 4 * feat]

    gkv = (gkv_ref[0] + gkvo_ref[0].astype(F32)).astype(BF)
    gq = gq_ref[0]
    da_ref[c, 0, 0:width] = nn(xt_sc[...], gkv).astype(BF)
    da_ref[1 - c, 0, 0:width, 0:feat] = nn(xt_sc[...], gq).astype(BF)
    da_ref[1 - c, 0, 0:width, feat : 2 * feat] = dwo_ref[0]
    sum_q = jnp.sum(gq.astype(F32), axis=0, keepdims=True)
    sum_q = jnp.concatenate((sum_q, jnp.zeros((1, feat), F32)), axis=1)
    sum_kv = jnp.sum(gkv.astype(F32), axis=0, keepdims=True)
    first = lax.broadcasted_iota(jnp.int32, (16, 1), 0) == 0
    da_ref[c, 0, edge] = jnp.where(first, sum_kv, sums_sc[...]).astype(BF)
    da_ref[1 - c, 0, edge] = jnp.where(first, sum_q, sums_sc[...]).astype(BF)
    acc_sc[...] += nt(gkv, wa_ref[c, 0]) + nt(gq, wa_ref[1 - c, 0, :, 0:feat])

    @pl.when(s == pl.num_programs(0) - 1)
    def _():
        gx_ref[...] = acc_sc[...].astype(BF)


def qkv_back_call(info, x, gq, gkv, gkvo, wa, dwo, g1, one, two):
    _, rows, width = x.shape
    slots, _, feat = gq.shape
    half = gkv.shape[2]
    blk = lambda r, w: spec((1, r, w), lambda i, info: (i, 0, 0))
    return pl.pallas_call(
        qkv_back_kernel,
        grid_spec=pltpu.PrefetchScalarGridSpec(
            num_scalar_prefetch=1,
            grid=(slots,),
            in_specs=[
                sequence(rows, width),
                blk(rows, feat),
                blk(rows, half),
                blk(rows, half),
                spec((2, 1, width, half), lambda i, info: (0, i, 0, 0)),
                blk(width, feat),
                whole((rows, width)),
                whole((8, width)),
                whole((8, width)),
            ],
            out_specs=[
                spec((2, 1, width + 16, half), lambda i, info: (0, i, 0, 0)),
                whole((rows, width)),
            ],
            scratch_shapes=[
                pltpu.VMEM((width, rows), BF),
                pltpu.VMEM((rows, width), F32),
                pltpu.VMEM((16, half), F32),
            ],
        ),
        out_shape=[
            jax.ShapeDtypeStruct((2, slots, width + 16, half), BF),
            jax.ShapeDtypeStruct((rows, width), BF),
        ],
        compiler_params=params(24),
        cost_estimate=cost(4 * rows * width * slots * 3 * feat, 2e7),
        name="qkv_back",
    )(info, x, gq, gkv, gkvo, wa, dwo, g1, one, two)


def shards_kernel(info, qkv_ref, out_ref, in_ref, down_ref, a_ref, b_ref, c_ref):
    feat = out_ref.shape[0]
    half = b_ref.shape[1]

    @pl.when(info[0] == 0)
    def _():
        a_ref[:, 0:feat] = qkv_ref[1]
        a_ref[:, feat:] = qkv_ref[2]
        b_ref[...] = in_ref[:, 0:half]
        c_ref[...] = down_ref[0:half, :].T

    @pl.when(info[0] == 1)
    def _():
        a_ref[:, 0:feat] = qkv_ref[0]
        a_ref[:, feat:] = out_ref[...].T
        b_ref[...] = in_ref[:, half:]
        c_ref[...] = down_ref[half:, :].T


def shards_call(info, qkv, out, win, down):
    rows, units = win.shape
    shape = jax.ShapeDtypeStruct((rows, units // 2), BF)
    return pl.pallas_call(
        shards_kernel,
        grid_spec=pltpu.PrefetchScalarGridSpec(
            num_scalar_prefetch=1,
            grid=(1,),
            in_specs=[whole(v.shape) for v in (qkv, out, win, down)],
            out_specs=[whole(shape.shape)] * 3,
        ),
        out_shape=[shape] * 3,
        compiler_params=params(8),
        cost_estimate=cost(0, 2e6),
        name="shards",
    )(info, qkv, out, win, down)


def wide_owned_kernel(info, own_ref, other_ref, in_ref, down_ref, din_ref):
    shard, units = in_ref.shape
    half = units // 2

    def write(first, second):
        for n, ref in enumerate((first, second)):
            cols = slice(n * half, (n + 1) * half)
            in_ref[:, cols] = ref[0:shard, :].astype(F32)
            din_ref[:, cols] = ref[shard : shard + 1, :].astype(F32)
            down_ref[cols, :] = ref[shard + 16 : 2 * shard + 16, :].astype(F32).T

    @pl.when(info[0] == 0)
    def _():
        write(own_ref, other_ref)

    @pl.when(info[0] == 1)
    def _():
        write(other_ref, own_ref)


def wide_owned_call(info, own, other):
    total, half = own.shape
    shard = (total - 16) // 2
    shapes = [(shard, 2 * half), (2 * half, shard), (1, 2 * half)]
    return pl.pallas_call(
        wide_owned_kernel,
        grid_spec=pltpu.PrefetchScalarGridSpec(
            num_scalar_prefetch=1,
            grid=(1,),
            in_specs=[whole((total, half))] * 2,
            out_specs=[whole(v) for v in shapes],
        ),
        out_shape=[jax.ShapeDtypeStruct(v, F32) for v in shapes],
        compiler_params=params(8),
        cost_estimate=cost(0, 2e6),
        name="wide_owned",
    )(info, own, other)


def owned_kernel(info, own_ref, other_ref, qkv_ref, out_ref, bias_ref, sums_ref):
    feat = out_ref.shape[0]
    shard = out_ref.shape[1]
    half = 2 * feat

    def write(first, second):
        qkv_ref[0] = second[0:shard, 0:feat].astype(F32)
        qkv_ref[1] = first[0:shard, 0:feat].astype(F32)
        qkv_ref[2] = first[0:shard, feat:].astype(F32)
        out_ref[...] = second[0:shard, feat:].astype(F32).T
        bias_ref[0:1, :] = second[shard : shard + 1, 0:feat].astype(F32)
        bias_ref[1:2, :] = first[shard : shard + 1, feat:].astype(F32)

    @pl.when(info[0] == 0)
    def _():
        write(own_ref, other_ref)

    @pl.when(info[0] == 1)
    def _():
        write(other_ref, own_ref)

    for n in range(6):
        at = shard + 1 + 2 * n
        sums_ref[n : n + 1, 0:half] = own_ref[at : at + 1, :].astype(F32)
        sums_ref[n : n + 1, half:] = own_ref[at + 1 : at + 2, :].astype(F32)


def owned_call(info, own, other):
    total, half = own.shape
    shard, feat = total - 16, half // 2
    shapes = [(3, shard, feat), (feat, shard), (2, feat), (6, 2 * half)]
    return pl.pallas_call(
        owned_kernel,
        grid_spec=pltpu.PrefetchScalarGridSpec(
            num_scalar_prefetch=1,
            grid=(1,),
            in_specs=[whole((total, half))] * 2,
            out_specs=[whole(v) for v in shapes],
        ),
        out_shape=[jax.ShapeDtypeStruct(v, F32) for v in shapes],
        compiler_params=params(8),
        cost_estimate=cost(0, 2e6),
        name="owned",
    )(info, own, other)


def ring(size, step):
    return [(i, (i + step) % size) for i in range(size)]


def tie(*values):
    return lax.optimization_barrier(values)


def swap(value):
    return lax.ppermute(value, "ctx", C_SWAP)


def by_x(value):
    return lax.ppermute(value, "tp", X_SWAP)


def by_y(value):
    return lax.ppermute(value, "tp", Y_SWAP)


def column_gather(shard, rank, size):
    if size > 4:
        return lax.all_gather(shard, "fsdp", axis=0, tiled=True)
    rows = shard.shape[0]
    full = jnp.zeros((size * rows,) + shard.shape[1:], shard.dtype)
    full = lax.dynamic_update_slice_in_dim(full, shard, rank * rows, 0)
    for step in range(1, size):
        got = lax.ppermute(shard, "fsdp", ring(size, step))
        full = lax.dynamic_update_slice_in_dim(full, got, ((rank - step) % size) * rows, 0)
    return full


def ring_sum(piece, rank, size):
    got = [piece(rank).astype(F32)]
    for step in range(1, size):
        got.append(lax.ppermute(piece((rank + step) % size), "fsdp", ring(size, step)).astype(F32))
    while len(got) > 1:
        cut = len(got) // 2
        got = [a + b for a, b in zip(got[:cut], got[cut:], strict=True)]
    return got[0].astype(BF)


def column_scatter(full, width, rank, size):
    rows = width // size
    extra = full[width:]
    if size > 4:
        own = lax.psum_scatter(full[:width], "fsdp", scatter_dimension=0, tiled=True)
        return jnp.concatenate((own, lax.psum(extra, "fsdp")), axis=0)

    def piece(owner):
        return jnp.concatenate(
            (lax.dynamic_slice_in_dim(full, owner * rows, rows, 0), extra), axis=0
        )

    return ring_sum(piece, rank, size)


def offload_gather(shard, size, pieces):
    full = lax.all_gather(shard, ("fsdp", "tp"), axis=0).reshape((size, 4) + shard.shape)
    if pieces == 1:
        full = full.transpose(1, 0, 2, 3).reshape(1, 4, size * shard.shape[0], shard.shape[1])
    return full


def offload_scatter(full, size):
    pieces, _, blocks, rows, half = full.shape
    if pieces == 1:
        full = full.reshape(2, blocks, size, rows // size, half).transpose(2, 0, 1, 3, 4)
    full = full.reshape(-1, half)
    return lax.psum_scatter(full, ("fsdp", "ctx", "tp"), scatter_dimension=0, tiled=True)


def plane_second(from_x, from_y):
    cut = from_x.shape[0] // 2
    return by_x(from_y[:cut]), by_y(from_x[cut:])


def add(a, b):
    return (a.astype(F32) + b.astype(F32)).astype(BF)


def scatter_first(blocks):
    cut = 384 if blocks.shape[1] > 384 else blocks.shape[1] // 2
    up, down = blocks[:, :cut], blocks[:, cut:]
    return up, down, by_x(jnp.stack((up[1], up[3]))), by_y(jnp.stack((down[2], down[3])))


def scatter_second(up, down, got_up, got_down):
    from_up = by_y(add(up[2], got_up[1]))
    from_down = by_x(add(down[1], got_down[1]))
    return add(up[0], got_up[0]), add(down[0], got_down[0]), from_up, from_down


def scatter_done(mid_up, mid_down, from_up, from_down):
    return jnp.concatenate((add(mid_up, from_up), add(mid_down, from_down)), axis=0)


def place_sequences(slots, index, dtype):
    out = jnp.zeros((len(slots),) + slots[0].shape, dtype)
    for distance, block in enumerate(slots):
        out = lax.dynamic_update_slice(out, block.astype(dtype)[None], (index ^ distance, 0, 0))
    return out


def per_device(
    tokens, lengths, qkv_weight, qv_bias, out_weight, out_bias, ffn_in, ffn_in_bias,
    ffn_out, ffn_out_bias, norm_gains, norm_shifts, cotangent,
):
    size = lax.axis_size("fsdp")
    rank = lax.axis_index("fsdp")
    c = lax.axis_index("ctx")
    t = lax.axis_index("tp")
    seqs, rows, width = tokens.shape
    assert lax.axis_size("tp") == 4 and lax.axis_size("ctx") == 2 and seqs == 4
    feat = qkv_weight.shape[2]
    units = ffn_in.shape[1]
    half = units // 2
    assert half == 2 * feat
    length = lax.dynamic_index_in_dim(lengths, t, 0, keepdims=False)
    info = jnp.stack((c.astype(jnp.int32), length, t.astype(jnp.int32)))

    shard_a, shard_b, shard_c = shards_call(info, qkv_weight, out_weight, ffn_in, ffn_out)
    pieces = size if shard_c.shape[0] % 16 == 0 else 1
    wc = offload_gather(shard_c, size, pieces)

    bias_own = jnp.concatenate((qv_bias.reshape(-1), ffn_in_bias)).reshape(1, -1)
    bias_x = by_x(bias_own)
    bias_y = by_y(bias_own)
    bias_x, shard_a = tie(bias_x, shard_a)
    bias_d = by_y(bias_x)
    col_a = column_gather(shard_a, rank, size)
    col_a, shard_b, bias_y, bias_d = tie(col_a, shard_b, bias_y, bias_d)
    ax, ay = by_x(col_a), by_y(col_a)
    col_b = column_gather(shard_b, rank, size)
    ax, ay = tie(ax, ay)
    au, al = plane_second(ax, ay)
    three = jnp.stack((col_a, ax, ay))
    three_other = swap(three)
    au, al, col_b = tie(au, al, col_b)
    last = jnp.concatenate((au, al), axis=0)[None]
    last_other = swap(last)
    bx, by = by_x(col_b), by_y(col_b)
    wa = jnp.concatenate((three, last, three_other, last_other), axis=0)
    wa = wa.reshape(2, 4, width, half)

    bias = jnp.stack((bias_own, bias_x, bias_y, bias_d))
    q_bias = bias[:, :, :feat]
    kv_bias = jnp.concatenate((jnp.zeros_like(q_bias), bias[:, :, feat : 2 * feat]), axis=2)
    in_bias = bias[:, :, 2 * feat :]
    swapped = jnp.concatenate((in_bias[:, :, half:], in_bias[:, :, :half]), axis=2)
    in_bias = jnp.where(c == 0, in_bias, swapped)
    zero_row = jnp.zeros_like(out_bias)
    vec = jnp.stack((out_bias, ffn_out_bias, norm_gains[0], norm_gains[1], norm_shifts[0], norm_shifts[1], zero_row, zero_row))

    q, kv = qkv_call(info, tokens, wa, q_bias, kv_bias)
    q, kv, bx, by = tie(q, kv, bx, by)
    kv_other = swap(kv)
    bu, bl = plane_second(bx, by)
    three_b = jnp.stack((col_b, bx, by))
    three_b_other = swap(three_b)
    context, lse = attn_call(info, q, kv, kv_other)
    context, lse, bu, bl, three_b_other = tie(context, lse, bu, bl, three_b_other)
    wc_other = swap(wc)
    last_b = jnp.concatenate((bu, bl), axis=0)[None]
    wb = jnp.concatenate((three_b, last_b, three_b_other, swap(last_b)), axis=0)
    wb = wb.reshape(2, 4, width, half)

    act, slope, nlow, hat, rstd, out, g_branch, g_r2, sums_two = ffn_call(
        info, context, wa, tokens, cotangent, vec, in_bias, wb, wc, wc_other
    )
    out_x, out_y = by_x(out), by_y(out)
    dc = down_call(info, g_branch, act, pieces)
    dc, g_branch = tie(dc, g_branch)
    own_c = offload_scatter(dc, size)
    db, g_r1, g_att, g_context, dwo, sums_one = ffn_back_call(
        info, g_branch, slope, wc, wc_other, wb, nlow, g_r2, hat, rstd, vec, wa, context
    )
    db, g_context, out_x, out_y = tie(db, g_context, out_x, out_y)
    out_u, out_l = plane_second(out_x, out_y)
    db_got = swap(db[1])
    gq1, gkv1, gkv_send1 = attn_back_call(info, q, kv, kv_other, lse, context, g_context, 0, 2)
    gq1, gkv1, gkv_send1, q, db_got, out_u, out_l = tie(
        gq1, gkv1, gkv_send1, q, db_got, out_u, out_l
    )
    part_b = scatter_first(add(db[0], db_got))
    gkv_got1 = swap(gkv_send1)
    gq2, gkv2, gkv_send2 = attn_back_call(info, q, kv, kv_other, lse, context, g_context, 2, 2)
    gq2, gkv2, gkv_send2, gkv_got1, *part_b = tie(gq2, gkv2, gkv_send2, gkv_got1, *part_b)
    part_b = scatter_second(*part_b)
    gkv_got2 = swap(gkv_send2)
    gq = jnp.concatenate((gq1, gq2), axis=0)
    gkv = jnp.concatenate((gkv1, gkv2), axis=0)
    gkv_got = jnp.concatenate((gkv_got1, gkv_got2), axis=0)
    da, g_tokens = qkv_back_call(
        info, tokens, gq, gkv, gkv_got, wa, dwo, g_r1, sums_one, sums_two
    )
    da, g_tokens, *part_b = tie(da, g_tokens, *part_b)
    da_got = swap(da[1])
    gt_x, gt_y = by_x(g_tokens), by_y(g_tokens)
    own_b = column_scatter(scatter_done(*part_b), width, rank, size)
    part_a = scatter_first(add(da[0], da_got))
    gt_x, gt_y, own_b = tie(gt_x, gt_y, own_b)
    gt_u, gt_l = plane_second(gt_x, gt_y)
    own_bc = jnp.concatenate((own_b, own_c), axis=0)
    other_bc = swap(own_bc)
    part_a = tie(*part_a)
    own_a = column_scatter(scatter_done(*scatter_second(*part_a)), width, rank, size)
    layer_output = place_sequences((out, out_x, out_y, jnp.concatenate((out_u, out_l), axis=0)), t, BF)
    grad_tokens = place_sequences(
        (g_tokens, gt_x, gt_y, jnp.concatenate((gt_u, gt_l), axis=0)), t, F32
    )
    grad_in, grad_down, d_in = wide_owned_call(info, own_bc, other_bc)
    grad_qkv, grad_out, d_qv, sums = owned_call(info, own_a, swap(own_a))
    return (
        layer_output,
        grad_tokens,
        grad_qkv,
        d_qv,
        grad_out,
        sums[2],
        grad_in,
        d_in[0],
        grad_down,
        sums[5],
        jnp.stack((sums[0], sums[3])),
        jnp.stack((sums[1], sums[4])),
    )


def solution(mesh):
    placed = (
        P("fsdp", "ctx", None),
        P("fsdp"),
        P(None, "fsdp", "tp"),
        P(None, "tp"),
        P("tp", "fsdp"),
        P(),
        P("fsdp", "tp"),
        P("tp"),
        P("tp", "fsdp"),
        P(),
        P(),
        P(),
        P("fsdp", "ctx", None),
    )
    return jax.shard_map(
        per_device,
        mesh=mesh,
        in_specs=placed,
        out_specs=(
            P("fsdp", "ctx", None),
            P("fsdp", "ctx", None),
            P(None, "fsdp", "tp"),
            P(None, "tp"),
            P("tp", "fsdp"),
            P(),
            P("fsdp", "tp"),
            P("tp"),
            P("tp", "fsdp"),
            P(),
            P(),
            P(),
        ),
        check_vma=False,
    )
```

```python
import functools
import math

import jax
import jax.numpy as jnp
from jax import lax
from jax.experimental import pallas as pl
from jax.experimental.pallas import tpu as pltpu
from jax.sharding import PartitionSpec as P

HD = 64
EPS = 1e-05
MASKED = -1000000000.0
LOG2E = math.log2(math.e)
SCALE = 0.125
BF = jnp.bfloat16
F32 = jnp.float32
MIB = 1024 * 1024

X_SWAP = [(0, 1), (1, 0), (2, 3), (3, 2)]
Y_SWAP = [(0, 2), (2, 0), (1, 3), (3, 1)]
C_SWAP = [(0, 1), (1, 0)]


def nn(a, b):
    return lax.dot_general(a, b, (((1,), (0,)), ((), ())), preferred_element_type=F32)


def nt(a, b):
    return lax.dot_general(a, b, (((1,), (1,)), ((), ())), preferred_element_type=F32)


def tn(a, b):
    return lax.dot_general(a, b, (((0,), (0,)), ((), ())), preferred_element_type=F32)


def params(mib):
    return pltpu.CompilerParams(
        dimension_semantics=("arbitrary",), vmem_limit_bytes=mib * MIB
    )


def cost(flops, moved, trans=0):
    return pl.CostEstimate(flops=int(flops), bytes_accessed=int(moved), transcendentals=int(trans))


def spec(shape, index):
    return pl.BlockSpec(shape, index)


def sequence(rows, width):
    return pl.BlockSpec((1, rows, width), lambda i, info: (info[2], 0, 0))


def whole(shape):
    zeros = (0,) * len(shape)
    return pl.BlockSpec(shape, lambda i, info: zeros)


def qkv_kernel(info, x_ref, a_ref, qb_ref, kvb_ref, q_ref, kv_ref):
    c = info[0]
    x = x_ref[0]
    kv_ref[0] = (nn(x, a_ref[c, 0]) + kvb_ref[0]).astype(BF)
    q_ref[0] = (nn(x, a_ref[1 - c, 0, :, 0 : q_ref.shape[2]]) + qb_ref[0]).astype(BF)


def qkv_call(info, x, wa, qb, kvb):
    _, rows, width = x.shape
    slots, half = wa.shape[1], wa.shape[3]
    feat = half // 2
    return pl.pallas_call(
        qkv_kernel,
        grid_spec=pltpu.PrefetchScalarGridSpec(
            num_scalar_prefetch=1,
            grid=(slots,),
            in_specs=[
                sequence(rows, width),
                spec((2, 1, width, half), lambda i, info: (0, i, 0, 0)),
                spec((1, 1, feat), lambda i, info: (i, 0, 0)),
                spec((1, 1, half), lambda i, info: (i, 0, 0)),
            ],
            out_specs=[
                spec((1, rows, feat), lambda i, info: (i, 0, 0)),
                spec((1, rows, half), lambda i, info: (i, 0, 0)),
            ],
        ),
        out_shape=[
            jax.ShapeDtypeStruct((slots, rows, feat), BF),
            jax.ShapeDtypeStruct((slots, rows, half), BF),
        ],
        compiler_params=params(12),
        cost_estimate=cost(2 * rows * width * slots * 3 * feat, 8e6),
        name="qkv",
    )(info, x, wa, qb, kvb)


def key_bias(info, rows, mine):
    owner = info[0] if mine else 1 - info[0]
    position = owner * rows + lax.broadcasted_iota(jnp.int32, (1, rows), 1)
    return jnp.where(position < info[1], 0.0, MASKED)


def attn_kernel(info, q_ref, kv_ref, kvo_ref, ctx_ref, lse_ref):
    rows, feat = q_ref.shape[1], q_ref.shape[2]
    bias_m, bias_o = key_bias(info, rows, True), key_bias(info, rows, False)
    lane = lax.broadcasted_iota(jnp.int32, (1, 128), 1)
    lse_all = jnp.zeros((rows, 128), F32)
    for h in range(feat // HD):
        cols = slice(h * HD, (h + 1) * HD)
        vcols = slice(feat + h * HD, feat + (h + 1) * HD)
        q = q_ref[0, :, cols]
        s_m = nt(q, kv_ref[0, :, cols]) * (SCALE * LOG2E) + bias_m
        s_o = nt(q, kvo_ref[0, :, cols]) * (SCALE * LOG2E) + bias_o
        top = jnp.maximum(
            jnp.max(s_m, axis=1, keepdims=True), jnp.max(s_o, axis=1, keepdims=True)
        )
        e_m = jnp.exp2(s_m - top)
        e_o = jnp.exp2(s_o - top)
        total = jnp.sum(e_m, axis=1, keepdims=True) + jnp.sum(e_o, axis=1, keepdims=True)
        out = nn(e_m.astype(BF), kv_ref[0, :, vcols]) + nn(e_o.astype(BF), kvo_ref[0, :, vcols])
        ctx_ref[0, :, cols] = (out * (1.0 / total)).astype(BF)
        lse_all = jnp.where(lane == h, top + jnp.log2(total), lse_all)
    lse_ref[0] = lse_all


def attn_call(info, q, kv, kvo):
    slots, rows, feat = q.shape
    half = kv.shape[2]
    blk = lambda w: spec((1, rows, w), lambda i, info: (i, 0, 0))
    heads = slots * feat // HD
    return pl.pallas_call(
        attn_kernel,
        grid_spec=pltpu.PrefetchScalarGridSpec(
            num_scalar_prefetch=1,
            grid=(slots,),
            in_specs=[blk(feat), blk(half), blk(half)],
            out_specs=[blk(feat), blk(128)],
        ),
        out_shape=[
            jax.ShapeDtypeStruct((slots, rows, feat), BF),
            jax.ShapeDtypeStruct((slots, rows, 128), F32),
        ],
        compiler_params=params(24),
        cost_estimate=cost(16 * rows * rows * 2 * HD * heads, 8e6, 2 * rows * rows * heads),
        name="attn",
    )(info, q, kv, kvo)


def attn_back_kernel(
    info, q_ref, kv_ref, kvo_ref, lse_ref, ctx_ref, g_ref, gq_ref, gkv_ref, gkvo_ref
):
    rows, feat = q_ref.shape[1], q_ref.shape[2]
    bias_m, bias_o = key_bias(info, rows, True), key_bias(info, rows, False)
    lane = lax.broadcasted_iota(jnp.int32, (1, 128), 1)
    lse_all = lse_ref[0]
    for h in range(feat // HD):
        cols = slice(h * HD, (h + 1) * HD)
        vcols = slice(feat + h * HD, feat + (h + 1) * HD)
        q, g = q_ref[0, :, cols], g_ref[0, :, cols]
        k_m, k_o = kv_ref[0, :, cols], kvo_ref[0, :, cols]
        lse = jnp.sum(jnp.where(lane == h, lse_all, 0.0), axis=1, keepdims=True)
        inner = jnp.sum(g.astype(F32) * ctx_ref[0, :, cols].astype(F32), axis=1, keepdims=True)
        p_m = jnp.exp2(nt(q, k_m) * (SCALE * LOG2E) + bias_m - lse)
        p_o = jnp.exp2(nt(q, k_o) * (SCALE * LOG2E) + bias_o - lse)
        gs_m = (p_m * (nt(g, kv_ref[0, :, vcols]) - inner)).astype(BF)
        gs_o = (p_o * (nt(g, kvo_ref[0, :, vcols]) - inner)).astype(BF)
        g_t, q_t = g.T, q.T
        gkv_ref[0, :, vcols] = nn(g_t, p_m.astype(BF)).T
        gkvo_ref[0, :, vcols] = nn(g_t, p_o.astype(BF)).T.astype(BF)
        gkv_ref[0, :, cols] = nn(q_t, gs_m).T * SCALE
        gkvo_ref[0, :, cols] = (nn(q_t, gs_o).T * SCALE).astype(BF)
        gq_ref[0, :, cols] = ((nn(gs_m, k_m) + nn(gs_o, k_o)) * SCALE).astype(BF)


def attn_back_call(info, q, kv, kvo, lse, ctx, g, first, slots):
    _, rows, feat = q.shape
    half = kv.shape[2]
    src = lambda w: spec((1, rows, w), lambda i, info: (i + first, 0, 0))
    blk = lambda w: spec((1, rows, w), lambda i, info: (i, 0, 0))
    heads = slots * feat // HD
    return pl.pallas_call(
        attn_back_kernel,
        grid_spec=pltpu.PrefetchScalarGridSpec(
            num_scalar_prefetch=1,
            grid=(slots,),
            in_specs=[src(feat), src(half), src(half), src(128), src(feat), src(feat)],
            out_specs=[blk(feat), blk(half), blk(half)],
        ),
        out_shape=[
            jax.ShapeDtypeStruct((slots, rows, feat), BF),
            jax.ShapeDtypeStruct((slots, rows, half), F32),
            jax.ShapeDtypeStruct((slots, rows, half), BF),
        ],
        compiler_params=params(24),
        cost_estimate=cost(160 * rows * rows * 2 * HD * heads, 12e6, 2 * rows * rows * heads),
        name="attn_back",
    )(info, q, kv, kvo, lse, ctx, g)


ROWS = 256


def wide(ref):
    return jnp.concatenate((ref[0, 0], ref[1, 0]), axis=1)


def gathered(own, other):
    join = lambda ref: ref[:, 0].reshape(ref.shape[0] * ref.shape[2], ref.shape[3])
    return jnp.concatenate((join(own), join(other)), axis=1)


def gathered_spec(array):
    pieces, _, rows, half = array.shape
    return pl.BlockSpec((pieces, 1, rows, half), lambda i, info: (0, info[2] ^ i, 0, 0))


def row_mask(info, rows, start, count):
    position = info[0] * rows + start + lax.broadcasted_iota(jnp.int32, (count, 1), 0)
    return (position < info[1]).astype(F32)


def ffn_kernel(
    info, ctx_ref, wo_ref, x_ref, cot_ref, vec_ref, bin_ref, wb_ref, wc_ref, wco_ref,
    act_ref, slope_ref, nlow_ref, hat_ref, rstd_ref, out_ref, gb_ref, gr_ref, sums_ref,
    normed_sc, branch_sc,
):
    k = pl.program_id(0)
    _, rows, width = x_ref.shape
    slots, feat = ctx_ref.shape[0], ctx_ref.shape[2]

    @pl.when(k == 0)
    def _():
        def chunk(n, carry):
            at = pl.ds(pl.multiple_of(n * ROWS, ROWS), ROWS)
            res = x_ref[0, at, :].astype(F32) + vec_ref[0:1, :]
            for s in range(slots):
                res += nt(ctx_ref[s, at, :], wo_ref[0, s, :, feat : 2 * feat])
            center = jnp.mean(res, axis=1, keepdims=True)
            res = res - center
            rstd = lax.rsqrt(jnp.mean(res * res, axis=1, keepdims=True) + EPS)
            hat = res * rstd
            normed = hat * vec_ref[2:3, :] + vec_ref[4:5, :]
            hat_ref[at, :] = hat
            rstd_ref[at, :] = jnp.broadcast_to(rstd, (ROWS, 128))
            normed_sc[at, :] = normed
            nlow_ref[at, :] = normed.astype(BF)
            return carry

        lax.fori_loop(0, rows // ROWS, chunk, 0)

    u = nn(nlow_ref[...], wide(wb_ref)) + bin_ref[0]
    cdf = 0.5 + 0.5 * lax.erf(u * math.sqrt(0.5))
    act = (u * cdf).astype(BF)
    act_ref[0] = act
    slope_ref[0] = cdf + u * (jnp.exp(u * u * -0.5) * (1.0 / math.sqrt(2.0 * math.pi)))
    part = nt(act, gathered(wc_ref, wco_ref))

    @pl.when(k == 0)
    def _():
        branch_sc[...] = part

    @pl.when(k > 0)
    def _():
        branch_sc[...] += part

    @pl.when(k == pl.num_programs(0) - 1)
    def _():
        def chunk(n, carry):
            s_gain, s_shift, s_bias = carry
            at = pl.ds(pl.multiple_of(n * ROWS, ROWS), ROWS)
            res = normed_sc[at, :] + branch_sc[at, :] + vec_ref[1:2, :]
            center = jnp.mean(res, axis=1, keepdims=True)
            res = res - center
            rstd = lax.rsqrt(jnp.mean(res * res, axis=1, keepdims=True) + EPS)
            hat = res * rstd
            out_ref[at, :] = (hat * vec_ref[3:4, :] + vec_ref[5:6, :]).astype(BF)
            g = cot_ref[0, at, :].astype(F32) * row_mask(info, rows, n * ROWS, ROWS)
            s_shift += jnp.sum(g, axis=0, keepdims=True)
            s_gain += jnp.sum(g * hat, axis=0, keepdims=True)
            gh = g * vec_ref[3:4, :]
            gr = rstd * (
                gh
                - jnp.mean(gh, axis=1, keepdims=True)
                - hat * jnp.mean(gh * hat, axis=1, keepdims=True)
            )
            gr_ref[at, :] = gr
            gb = gr.astype(BF)
            gb_ref[at, :] = gb
            s_bias += jnp.sum(gb.astype(F32), axis=0, keepdims=True)
            return s_gain, s_shift, s_bias

        zero = jnp.zeros((1, width), F32)
        s_gain, s_shift, s_bias = lax.fori_loop(0, rows // ROWS, chunk, (zero, zero, zero))
        sums_ref[0:1, :] = s_gain
        sums_ref[1:2, :] = s_shift
        sums_ref[2:3, :] = s_bias
        sums_ref[3:8, :] = jnp.zeros((5, width), F32)


def ffn_call(info, ctx, wa, x, cot, vec, b_in, wb, wc, wco):
    slots, rows, feat = ctx.shape
    width = x.shape[2]
    blocks, half = wb.shape[1], wb.shape[3]
    units = 2 * half
    kblk = lambda r, w: spec((1, r, w), lambda i, info: (i, 0, 0))
    wblk = spec((2, 1, width, half), lambda i, info: (0, i, 0, 0))
    return pl.pallas_call(
        ffn_kernel,
        grid_spec=pltpu.PrefetchScalarGridSpec(
            num_scalar_prefetch=1,
            grid=(blocks,),
            in_specs=[
                whole((slots, rows, feat)),
                spec((1, slots, width, half), lambda i, info: (1 - info[0], 0, 0, 0)),
                sequence(rows, width),
                sequence(rows, width),
                whole((8, width)),
                kblk(1, units),
                wblk,
                gathered_spec(wc),
                gathered_spec(wco),
            ],
            out_specs=[
                kblk(rows, units),
                kblk(rows, units),
                whole((rows, width)),
                whole((rows, width)),
                whole((rows, 128)),
                whole((rows, width)),
                whole((rows, width)),
                whole((rows, width)),
                whole((8, width)),
            ],
            scratch_shapes=[pltpu.VMEM((rows, width), F32), pltpu.VMEM((rows, width), F32)],
        ),
        out_shape=[
            jax.ShapeDtypeStruct((blocks, rows, units), BF),
            jax.ShapeDtypeStruct((blocks, rows, units), F32),
            jax.ShapeDtypeStruct((rows, width), BF),
            jax.ShapeDtypeStruct((rows, width), F32),
            jax.ShapeDtypeStruct((rows, 128), F32),
            jax.ShapeDtypeStruct((rows, width), BF),
            jax.ShapeDtypeStruct((rows, width), BF),
            jax.ShapeDtypeStruct((rows, width), F32),
            jax.ShapeDtypeStruct((8, width), F32),
        ],
        compiler_params=params(28),
        cost_estimate=cost(12 * rows * width * blocks * units, 3e7, 2 * rows * blocks * units),
        name="ffn",
    )(info, ctx, wa, x, cot, vec, b_in, wb, wc, wco)


def down_kernel(info, gb_ref, act_ref, dc_ref, gt_sc):
    @pl.when(pl.program_id(0) == 0)
    def _():
        gt_sc[...] = gb_ref[...].T

    grad = nn(gt_sc[...], act_ref[0]).astype(BF)
    pieces, _, _, rows, half = dc_ref.shape
    c = info[0]
    for n in range(pieces):
        dc_ref[n, c, 0] = grad[n * rows : (n + 1) * rows, :half]
        dc_ref[n, 1 - c, 0] = grad[n * rows : (n + 1) * rows, half:]


def down_call(info, gb, act, pieces):
    rows, width = gb.shape
    blocks, _, units = act.shape
    shape = (pieces, 2, blocks, width // pieces, units // 2)
    return pl.pallas_call(
        down_kernel,
        grid_spec=pltpu.PrefetchScalarGridSpec(
            num_scalar_prefetch=1,
            grid=(blocks,),
            in_specs=[whole((rows, width)), spec((1, rows, units), lambda i, info: (i, 0, 0))],
            out_specs=spec(
                shape[:2] + (1,) + shape[3:], lambda i, info: (0, 0, info[2] ^ i, 0, 0)
            ),
            scratch_shapes=[pltpu.VMEM((width, rows), BF)],
        ),
        out_shape=jax.ShapeDtypeStruct(shape, BF),
        compiler_params=params(16),
        cost_estimate=cost(2 * rows * width * blocks * units, 9e6),
        name="down_grad",
    )(info, gb, act)


def ffn_back_kernel(
    info, gb_ref, slope_ref, wc_ref, wco_ref, wb_ref, nlow_ref, gr_ref, hat_ref, rstd_ref, vec_ref, wo_ref, ctx_ref,
    own_ref, other_ref, g1_ref, gatt_ref, gctx_ref, dwo_ref, sums_ref,
    nt_sc, acc_sc,
):
    k = pl.program_id(0)
    rows, width = gb_ref.shape
    half = wb_ref.shape[3]
    slots, feat = ctx_ref.shape[0], ctx_ref.shape[2]

    @pl.when(k == 0)
    def _():
        nt_sc[...] = nlow_ref[...].T

    gh = (slope_ref[0] * nn(gb_ref[...], gathered(wc_ref, wco_ref))).astype(BF)
    part = nt(gh, wide(wb_ref))

    @pl.when(k == 0)
    def _():
        acc_sc[...] = part

    @pl.when(k > 0)
    def _():
        acc_sc[...] += part

    total = jnp.broadcast_to(jnp.sum(gh.astype(F32), axis=0, keepdims=True), (16, 2 * half))
    total = total.astype(BF)
    grad = nn(nt_sc[...], gh).astype(BF)
    for n, ref in enumerate((own_ref, other_ref)):
        ref[0, 0:width] = grad[:, n * half : (n + 1) * half]
        ref[0, width : width + 16] = total[:, n * half : (n + 1) * half]

    @pl.when(k == pl.num_programs(0) - 1)
    def _():
        def chunk(n, carry):
            s_gain, s_shift, s_bias = carry
            at = pl.ds(pl.multiple_of(n * ROWS, ROWS), ROWS)
            g = acc_sc[at, :] + gr_ref[at, :]
            hat = hat_ref[at, :]
            s_shift += jnp.sum(g, axis=0, keepdims=True)
            s_gain += jnp.sum(g * hat, axis=0, keepdims=True)
            gh = g * vec_ref[2:3, :]
            g1 = rstd_ref[at, 0:1] * (
                gh
                - jnp.mean(gh, axis=1, keepdims=True)
                - hat * jnp.mean(gh * hat, axis=1, keepdims=True)
            )
            g1_ref[at, :] = g1
            gatt = g1.astype(BF)
            gatt_ref[at, :] = gatt
            s_bias += jnp.sum(gatt.astype(F32), axis=0, keepdims=True)
            for s in range(slots):
                gctx_ref[s, at, :] = nn(gatt, wo_ref[0, s, :, feat : 2 * feat]).astype(BF)
            return s_gain, s_shift, s_bias

        zero = jnp.zeros((1, width), F32)
        s_gain, s_shift, s_bias = lax.fori_loop(0, rows // ROWS, chunk, (zero, zero, zero))
        sums_ref[0:1, :] = s_gain
        sums_ref[1:2, :] = s_shift
        sums_ref[2:3, :] = s_bias
        sums_ref[3:8, :] = jnp.zeros((5, width), F32)
        nt_sc[...] = gatt_ref[...].T
        for s in range(slots):
            dwo_ref[s] = nn(nt_sc[...], ctx_ref[s]).astype(BF)


def ffn_back_call(info, gb, slope, wc, wco, wb, nlow, gr, hat, rstd, vec, wa, ctx):
    slots, rows, feat = ctx.shape
    width = gb.shape[1]
    blocks, half = wb.shape[1], wb.shape[3]
    return pl.pallas_call(
        ffn_back_kernel,
        grid_spec=pltpu.PrefetchScalarGridSpec(
            num_scalar_prefetch=1,
            grid=(blocks,),
            in_specs=[
                whole((rows, width)),
                spec((1, rows, 2 * half), lambda i, info: (i, 0, 0)),
                gathered_spec(wc),
                gathered_spec(wco),
                spec((2, 1, width, half), lambda i, info: (0, i, 0, 0)),
                whole((rows, width)),
                whole((rows, width)),
                whole((rows, width)),
                whole((rows, 128)),
                whole((8, width)),
                spec((1, slots, width, half), lambda i, info: (1 - info[0], 0, 0, 0)),
                whole((slots, rows, feat)),
            ],
            out_specs=[
                spec((1, width + 16, half), lambda i, info: (i, 0, 0)),
                spec((1, width + 16, half), lambda i, info: (i, 0, 0)),
                whole((rows, width)),
                whole((rows, width)),
                whole((slots, rows, feat)),
                whole((slots, width, feat)),
                whole((8, width)),
            ],
            scratch_shapes=[
                pltpu.VMEM((width, rows), BF),
                pltpu.VMEM((rows, width), F32),
            ],
        ),
        out_shape=[
            jax.ShapeDtypeStruct((blocks, width + 16, half), BF),
            jax.ShapeDtypeStruct((blocks, width + 16, half), BF),
            jax.ShapeDtypeStruct((rows, width), F32),
            jax.ShapeDtypeStruct((rows, width), BF),
            jax.ShapeDtypeStruct((slots, rows, feat), BF),
            jax.ShapeDtypeStruct((slots, width, feat), BF),
            jax.ShapeDtypeStruct((8, width), F32),
        ],
        compiler_params=params(36),
        cost_estimate=cost(48 * rows * width * blocks * half, 3e7),
        name="ffn_back",
    )(info, gb, slope, wc, wco, wb, nlow, gr, hat, rstd, vec, wa, ctx)


def qkv_back_kernel(
    info, x_ref, gq_ref, gkv_ref, gkvo_ref, wa_ref, dwo_ref, g1_ref, one_ref, two_ref,
    da_ref, gx_ref, xt_sc, acc_sc, sums_sc,
):
    s = pl.program_id(0)
    c = info[0]
    width = x_ref.shape[2]
    feat = gq_ref.shape[2]
    edge = slice(width, width + 16)

    @pl.when(s == 0)
    def _():
        xt_sc[...] = x_ref[0].T
        acc_sc[...] = g1_ref[...]
        sums_sc[...] = jnp.zeros_like(sums_sc)
        for n in range(3):
            for m, ref in enumerate((one_ref, two_ref)):
                at = 1 + 2 * (3 * m + n)
                sums_sc[at : at + 1] = ref[n : n + 1, 0 : 2 * feat]
                sums_sc[at + 1 : at + 2] = ref[n : n + 1, 2 * feat : 4 * feat]

    gkv = (gkv_ref[0] + gkvo_ref[0].astype(F32)).astype(BF)
    gq = gq_ref[0]
    da_ref[c, 0, 0:width] = nn(xt_sc[...], gkv).astype(BF)
    da_ref[1 - c, 0, 0:width, 0:feat] = nn(xt_sc[...], gq).astype(BF)
    da_ref[1 - c, 0, 0:width, feat : 2 * feat] = dwo_ref[0]
    sum_q = jnp.sum(gq.astype(F32), axis=0, keepdims=True)
    sum_q = jnp.concatenate((sum_q, jnp.zeros((1, feat), F32)), axis=1)
    sum_kv = jnp.sum(gkv.astype(F32), axis=0, keepdims=True)
    first = lax.broadcasted_iota(jnp.int32, (16, 1), 0) == 0
    da_ref[c, 0, edge] = jnp.where(first, sum_kv, sums_sc[...]).astype(BF)
    da_ref[1 - c, 0, edge] = jnp.where(first, sum_q, sums_sc[...]).astype(BF)
    acc_sc[...] += nt(gkv, wa_ref[c, 0]) + nt(gq, wa_ref[1 - c, 0, :, 0:feat])

    @pl.when(s == pl.num_programs(0) - 1)
    def _():
        gx_ref[...] = acc_sc[...].astype(BF)


def qkv_back_call(info, x, gq, gkv, gkvo, wa, dwo, g1, one, two):
    _, rows, width = x.shape
    slots, _, feat = gq.shape
    half = gkv.shape[2]
    blk = lambda r, w: spec((1, r, w), lambda i, info: (i, 0, 0))
    return pl.pallas_call(
        qkv_back_kernel,
        grid_spec=pltpu.PrefetchScalarGridSpec(
            num_scalar_prefetch=1,
            grid=(slots,),
            in_specs=[
                sequence(rows, width),
                blk(rows, feat),
                blk(rows, half),
                blk(rows, half),
                spec((2, 1, width, half), lambda i, info: (0, i, 0, 0)),
                blk(width, feat),
                whole((rows, width)),
                whole((8, width)),
                whole((8, width)),
            ],
            out_specs=[
                spec((2, 1, width + 16, half), lambda i, info: (0, i, 0, 0)),
                whole((rows, width)),
            ],
            scratch_shapes=[
                pltpu.VMEM((width, rows), BF),
                pltpu.VMEM((rows, width), F32),
                pltpu.VMEM((16, half), F32),
            ],
        ),
        out_shape=[
            jax.ShapeDtypeStruct((2, slots, width + 16, half), BF),
            jax.ShapeDtypeStruct((rows, width), BF),
        ],
        compiler_params=params(24),
        cost_estimate=cost(16 * rows * width * slots * 3 * feat, 2e7),
        name="qkv_back",
    )(info, x, gq, gkv, gkvo, wa, dwo, g1, one, two)


def shards_kernel(info, qkv_ref, out_ref, in_ref, down_ref, a_ref, b_ref, c_ref):
    feat = out_ref.shape[0]
    half = b_ref.shape[1]

    @pl.when(info[0] == 0)
    def _():
        a_ref[:, 0:feat] = qkv_ref[1]
        a_ref[:, feat:] = qkv_ref[2]
        b_ref[...] = in_ref[:, 0:half]
        c_ref[...] = down_ref[0:half, :].T

    @pl.when(info[0] == 1)
    def _():
        a_ref[:, 0:feat] = qkv_ref[0]
        a_ref[:, feat:] = out_ref[...].T
        b_ref[...] = in_ref[:, half:]
        c_ref[...] = down_ref[half:, :].T


def shards_call(info, qkv, out, win, down):
    rows, units = win.shape
    shape = jax.ShapeDtypeStruct((rows, units // 2), BF)
    return pl.pallas_call(
        shards_kernel,
        grid_spec=pltpu.PrefetchScalarGridSpec(
            num_scalar_prefetch=1,
            grid=(1,),
            in_specs=[whole(v.shape) for v in (qkv, out, win, down)],
            out_specs=[whole(shape.shape)] * 3,
        ),
        out_shape=[shape] * 3,
        compiler_params=params(8),
        cost_estimate=cost(0, 2e6),
        name="shards",
    )(info, qkv, out, win, down)


def owned_kernel(
    info, own_ref, other_ref, qkv_ref, out_ref, bias_ref, sums_ref, in_ref, down_ref, din_ref
):
    feat = out_ref.shape[0]
    shard = out_ref.shape[1]
    half = 2 * feat

    def write(first, second):
        qkv_ref[0] = second[0:shard, 0:feat].astype(F32)
        qkv_ref[1] = first[0:shard, 0:feat].astype(F32)
        qkv_ref[2] = first[0:shard, feat:].astype(F32)
        out_ref[...] = second[0:shard, feat:].astype(F32).T
        bias_ref[0:1, :] = second[shard : shard + 1, 0:feat].astype(F32)
        bias_ref[1:2, :] = first[shard : shard + 1, feat:].astype(F32)
        at = shard + 16
        for n, ref in enumerate((first, second)):
            cols = slice(n * half, (n + 1) * half)
            in_ref[:, cols] = ref[at : at + shard, :].astype(F32)
            din_ref[:, cols] = ref[at + shard : at + shard + 1, :].astype(F32)
            down_ref[cols, :] = ref[2 * at : 2 * at + shard, :].astype(F32).T

    @pl.when(info[0] == 0)
    def _():
        write(own_ref, other_ref)

    @pl.when(info[0] == 1)
    def _():
        write(other_ref, own_ref)

    for n in range(6):
        at = shard + 1 + 2 * n
        sums_ref[n : n + 1, 0:half] = own_ref[at : at + 1, :].astype(F32)
        sums_ref[n : n + 1, half:] = own_ref[at + 1 : at + 2, :].astype(F32)


def owned_call(info, own, other):
    total, half = own.shape
    shard, feat = (total - 32) // 3, half // 2
    shapes = [(3, shard, feat), (feat, shard), (2, feat), (6, 2 * half)]
    shapes += [(shard, 2 * half), (2 * half, shard), (1, 2 * half)]
    return pl.pallas_call(
        owned_kernel,
        grid_spec=pltpu.PrefetchScalarGridSpec(
            num_scalar_prefetch=1,
            grid=(1,),
            in_specs=[whole((total, half))] * 2,
            out_specs=[whole(v) for v in shapes],
        ),
        out_shape=[jax.ShapeDtypeStruct(v, F32) for v in shapes],
        compiler_params=params(8),
        cost_estimate=cost(0, 2e6),
        name="owned",
    )(info, own, other)


def ring(size, step):
    return [(i, (i + step) % size) for i in range(size)]


def tie(*values):
    return lax.optimization_barrier(values)


def swap(value):
    return lax.ppermute(value, "ctx", C_SWAP)


def by_x(value):
    return lax.ppermute(value, "tp", X_SWAP)


def by_y(value):
    return lax.ppermute(value, "tp", Y_SWAP)


def column_gather(shard, rank, size):
    if size > 4:
        return lax.all_gather(shard, "fsdp", axis=0, tiled=True)
    rows = shard.shape[0]
    full = jnp.zeros((size * rows,) + shard.shape[1:], shard.dtype)
    full = lax.dynamic_update_slice_in_dim(full, shard, rank * rows, 0)
    for step in range(1, size):
        got = lax.ppermute(shard, "fsdp", ring(size, step))
        full = lax.dynamic_update_slice_in_dim(full, got, ((rank - step) % size) * rows, 0)
    return full


def column_parts(full, width, rank, size):
    rows = width // size
    extra = full[width:]
    if size > 4:
        own = lax.psum_scatter(full[:width], "fsdp", scatter_dimension=0, tiled=True)
        return [jnp.concatenate((own, lax.psum(extra, "fsdp")), axis=0)]

    def piece(owner):
        return jnp.concatenate(
            (lax.dynamic_slice_in_dim(full, owner * rows, rows, 0), extra), axis=0
        )

    parts = [piece(rank)]
    for step in range(1, size):
        parts.append(lax.ppermute(piece((rank + step) % size), "fsdp", ring(size, step)))
    return parts


def column_sum(parts, size):
    got = [part.astype(F32) for part in parts]
    while len(got) > 1:
        cut = len(got) // 2
        got = [a + b for a, b in zip(got[:cut], got[cut:], strict=True)]
    return got[0].astype(BF)


def offload_gather(shard, size, pieces):
    full = lax.all_gather(shard, ("fsdp", "tp"), axis=0).reshape((size, 4) + shard.shape)
    if pieces == 1:
        full = full.transpose(1, 0, 2, 3).reshape(1, 4, size * shard.shape[0], shard.shape[1])
    return full


def offload_scatter(full, size):
    pieces, _, blocks, rows, half = full.shape
    if pieces == 1:
        full = full.reshape(2, blocks, size, rows // size, half).transpose(2, 0, 1, 3, 4)
    full = full.reshape(-1, half)
    return lax.psum_scatter(full, ("fsdp", "ctx", "tp"), scatter_dimension=0, tiled=True)


def plane_second(from_x, from_y):
    cut = from_x.shape[0] // 2
    return by_x(from_y[:cut]), by_y(from_x[cut:])


def add(a, b):
    return (a.astype(F32) + b.astype(F32)).astype(BF)


def scatter_first(blocks):
    cut = 384 if blocks.shape[1] > 384 else blocks.shape[1] // 2
    up, down = blocks[:, :cut], blocks[:, cut:]
    return up, down, by_x(jnp.stack((up[1], up[3]))), by_y(jnp.stack((down[2], down[3])))


def scatter_second(up, down, got_up, got_down):
    from_up = by_y(add(up[2], got_up[1]))
    from_down = by_x(add(down[1], got_down[1]))
    return add(up[0], got_up[0]), add(down[0], got_down[0]), from_up, from_down


def scatter_done(mid_up, mid_down, from_up, from_down):
    return jnp.concatenate((add(mid_up, from_up), add(mid_down, from_down)), axis=0)


def place_sequences(slots, index, dtype):
    out = jnp.zeros((len(slots),) + slots[0].shape, dtype)
    for distance, block in enumerate(slots):
        out = lax.dynamic_update_slice(out, block.astype(dtype)[None], (index ^ distance, 0, 0))
    return out


def per_device(
    tokens, lengths, qkv_weight, qv_bias, out_weight, out_bias, ffn_in, ffn_in_bias,
    ffn_out, ffn_out_bias, norm_gains, norm_shifts, cotangent,
):
    size = lax.axis_size("fsdp")
    rank = lax.axis_index("fsdp")
    c = lax.axis_index("ctx")
    t = lax.axis_index("tp")
    seqs, rows, width = tokens.shape
    assert lax.axis_size("tp") == 4 and lax.axis_size("ctx") == 2 and seqs == 4
    feat = qkv_weight.shape[2]
    units = ffn_in.shape[1]
    half = units // 2
    assert half == 2 * feat
    length = lax.dynamic_index_in_dim(lengths, t, 0, keepdims=False)
    info = jnp.stack((c.astype(jnp.int32), length, t.astype(jnp.int32)))

    shard_a, shard_b, shard_c = shards_call(info, qkv_weight, out_weight, ffn_in, ffn_out)
    pieces = size if shard_c.shape[0] % 16 == 0 else 1
    wc = offload_gather(shard_c, size, pieces)

    bias_own = jnp.concatenate((qv_bias.reshape(-1), ffn_in_bias)).reshape(1, -1)
    bias_x = by_x(bias_own)
    bias_y = by_y(bias_own)
    bias_x, shard_a = tie(bias_x, shard_a)
    bias_d = by_y(bias_x)
    col_a = column_gather(shard_a, rank, size)
    col_a, shard_b, bias_y, bias_d = tie(col_a, shard_b, bias_y, bias_d)
    ax, ay = by_x(col_a), by_y(col_a)
    col_b = column_gather(shard_b, rank, size)
    ax, ay = tie(ax, ay)
    au, al = plane_second(ax, ay)
    three = jnp.stack((col_a, ax, ay))
    three_other = swap(three)
    au, al, col_b = tie(au, al, col_b)
    last = jnp.concatenate((au, al), axis=0)[None]
    last_other = swap(last)
    bx, by = by_x(col_b), by_y(col_b)
    wa = jnp.concatenate((three, last, three_other, last_other), axis=0)
    wa = wa.reshape(2, 4, width, half)

    bias = jnp.stack((bias_own, bias_x, bias_y, bias_d))
    q_bias = bias[:, :, :feat]
    kv_bias = jnp.concatenate((jnp.zeros_like(q_bias), bias[:, :, feat : 2 * feat]), axis=2)
    in_bias = bias[:, :, 2 * feat :]
    swapped = jnp.concatenate((in_bias[:, :, half:], in_bias[:, :, :half]), axis=2)
    in_bias = jnp.where(c == 0, in_bias, swapped)
    zero_row = jnp.zeros_like(out_bias)
    vec = jnp.stack((out_bias, ffn_out_bias, norm_gains[0], norm_gains[1], norm_shifts[0], norm_shifts[1], zero_row, zero_row))

    q, kv = qkv_call(info, tokens, wa, q_bias, kv_bias)
    kv_other = swap(kv)
    context, lse = attn_call(info, q, kv, kv_other)
    lse, bx, by = tie(lse, bx, by)
    bu, bl = plane_second(bx, by)
    three_b = jnp.stack((col_b, bx, by))
    three_b_other = swap(three_b)
    last_b = jnp.concatenate((bu, bl), axis=0)[None]
    wb = jnp.concatenate((three_b, last_b, three_b_other, swap(last_b)), axis=0)
    wb, wc = tie(wb.reshape(2, 4, width, half), wc)
    wc_other = swap(wc)

    act, slope, nlow, hat, rstd, out, g_branch, g_r2, sums_two = ffn_call(
        info, context, wa, tokens, cotangent, vec, in_bias, wb, wc, wc_other
    )
    out_x, out_y = by_x(out), by_y(out)
    dc = down_call(info, g_branch, act, pieces)
    dc, g_branch = tie(dc, g_branch)
    own_c = offload_scatter(dc, size)
    db, db_send, g_r1, g_att, g_context, dwo, sums_one = ffn_back_call(
        info, g_branch, slope, wc, wc_other, wb, nlow, g_r2, hat, rstd, vec, wa, context
    )
    db, db_send, g_context, out_x, out_y = tie(db, db_send, g_context, out_x, out_y)
    out_u, out_l = plane_second(out_x, out_y)
    db_got = swap(db_send)
    gq1, gkv1, gkv_send1 = attn_back_call(info, q, kv, kv_other, lse, context, g_context, 0, 2)
    gq1, gkv1, gkv_send1, q, db_got, out_u, out_l = tie(
        gq1, gkv1, gkv_send1, q, db_got, out_u, out_l
    )
    part_b = scatter_first(add(db, db_got))
    gkv_got1 = swap(gkv_send1)
    gq2, gkv2, gkv_send2 = attn_back_call(info, q, kv, kv_other, lse, context, g_context, 2, 2)
    gq2, gkv2, gkv_send2, gkv_got1 = tie(gq2, gkv2, gkv_send2, gkv_got1)
    gkv_got2 = swap(gkv_send2)
    gq = jnp.concatenate((gq1, gq2), axis=0)
    gkv = jnp.concatenate((gkv1, gkv2), axis=0)
    gkv_got = jnp.concatenate((gkv_got1, gkv_got2), axis=0)
    da, g_tokens = qkv_back_call(
        info, tokens, gq, gkv, gkv_got, wa, dwo, g_r1, sums_one, sums_two
    )
    da, g_tokens, *part_b = tie(da, g_tokens, *part_b)
    da_got = swap(da[1])
    part_b = scatter_second(*part_b)
    part_a = scatter_first(add(da[0], da_got))
    parts = tie(*part_a, *part_b)
    part_a = tie(*scatter_second(*parts[:4]))
    ring_b = column_parts(scatter_done(*parts[4:]), width, rank, size)
    full_a, g_tokens, own_c, *ring_b = tie(scatter_done(*part_a), g_tokens, own_c, *ring_b)
    ring_a = column_parts(full_a, width, rank, size)
    gt_x, gt_y = by_x(g_tokens), by_y(g_tokens)
    own_b = column_sum(ring_b, size)
    gt_x, gt_y, *ring_a = tie(gt_x, gt_y, *ring_a)
    gt_u, gt_l = plane_second(gt_x, gt_y)
    own = jnp.concatenate((column_sum(ring_a, size), own_b, own_c), axis=0)
    other = swap(own)
    layer_output = place_sequences((out, out_x, out_y, jnp.concatenate((out_u, out_l), axis=0)), t, BF)
    grad_tokens = place_sequences(
        (g_tokens, gt_x, gt_y, jnp.concatenate((gt_u, gt_l), axis=0)), t, F32
    )
    grad_qkv, grad_out, d_qv, sums, grad_in, grad_down, d_in = owned_call(info, own, other)
    return (
        layer_output,
        grad_tokens,
        grad_qkv,
        d_qv,
        grad_out,
        sums[2],
        grad_in,
        d_in[0],
        grad_down,
        sums[5],
        jnp.stack((sums[0], sums[3])),
        jnp.stack((sums[1], sums[4])),
    )


def solution(mesh):
    placed = (
        P("fsdp", "ctx", None),
        P("fsdp"),
        P(None, "fsdp", "tp"),
        P(None, "tp"),
        P("tp", "fsdp"),
        P(),
        P("fsdp", "tp"),
        P("tp"),
        P("tp", "fsdp"),
        P(),
        P(),
        P(),
        P("fsdp", "ctx", None),
    )
    return jax.shard_map(
        per_device,
        mesh=mesh,
        in_specs=placed,
        out_specs=(
            P("fsdp", "ctx", None),
            P("fsdp", "ctx", None),
            P(None, "fsdp", "tp"),
            P(None, "tp"),
            P("tp", "fsdp"),
            P(),
            P("fsdp", "tp"),
            P("tp"),
            P("tp", "fsdp"),
            P(),
            P(),
            P(),
        ),
        check_vma=False,
    )
```
